32 devices in a mesh: group: 2 (over y), clip: 4 (over z), pix: 4 (over x, core).
Axes of the slice: x: 2, y: 2, z: 4, core: 2. Of those that a mesh axis runs over, the one named last changes fastest.
Arguments:
- latents: bfloat16 [64, 256, 320], P(('group', 'clip'), 'pix'), parts along dimension 0, may hold values from -6 to 6
- sampled: int32 [8], P(('group', 'clip')), parts along dimension 0, may hold values from 0 to 7
- temporal_gain: float32 [320], replicated, may hold values from 0.5 to 1.5
- temporal_qkv: bfloat16 [320, 960], replicated, may hold values from -64 to 64
- temporal_out: bfloat16 [320, 320], replicated, may hold values from -0.3125 to 0.3125
- spatial_gain: float32 [320], replicated, may hold values from 0.5 to 1.5
- spatial_qkv: bfloat16 [320, 960], replicated, may hold values from -64 to 64
- spatial_out: bfloat16 [320, 320], replicated, may hold values from -0.3125 to 0.3125
Outputs:
- refined: bfloat16 [64, 256, 320], P(('group', 'clip', 'pix')), parts along dimension 0
The draws below stay inside these ranges and needn't reach their ends.
There are 2 independent parts, one for each index of `group`. The reference program is written for one: setup_inputs(seed, part) draws one part's arguments, and reference() takes and returns one part's arrays. A program takes and returns all parts, laid end to end along the dimension named above; an argument that names none is the same for every part. Nothing has to cross between parts.
All inputs are finite; a program needn't handle non-finite values.
Results may differ from the reference program's by a relative error of at most 0.014.
The reference program's roundings to bfloat16 on the way count: a program that leaves them out, or rounds other values in their place, can miss the bound.
Values may be sent and summed in bfloat16 or wider, within the bound.
No kernel may reach another device: no remote copies, remote signals or barrier semaphores. Data moves between devices by JAX's collectives and lax.ppermute only.
A program may use at most 64 MiB of HBM per device.

```python
import math
import jax
import jax.numpy as jnp
from jax import lax

WIDTH = 320
HEADS = 5
HEAD_DIM = 64
FPC = 8
HALO = 4
CLIPS = 4
FRAMES = 32
PIX = 256


def qkv_entries(key, salt):
    base_key = jax.random.fold_in(key, salt)
    normal_key = jax.random.fold_in(base_key, 1)
    entries = jnp.clip(jax.random.normal(normal_key, (WIDTH, 3 * WIDTH), jnp.float32), -4.0, 4.0) * WIDTH ** (-0.5)
    return entries.astype(jnp.bfloat16)


def draw_temporal_qkv(key, part):
    return qkv_entries(key, 11)


def draw_spatial_qkv(key, part):
    return qkv_entries(key, 23)


def set_ends(values, own_key, least, top_value):
    longest = values.shape.index(max(values.shape))
    spots = []
    for shift in (0, 1):
        where = [jax.random.randint(jax.random.fold_in(own_key, axis), (), 0, length) for axis, length in enumerate(values.shape)]
        where[longest] = (where[longest] + shift) % values.shape[longest]
        spots.append(tuple(where))
    return values.at[spots[0]].set(least).at[spots[1]].set(top_value)


def level_of(own_key, extent, pieces, smallest, top_value):
    def one(position, parts):
        steps = jax.random.uniform(jax.random.fold_in(jax.random.fold_in(own_key, 6), position), (parts,), jnp.float32, smallest / len(pieces), top_value / len(pieces))
        return jnp.repeat(jnp.exp(steps), extent[position] // parts).reshape((-1,) + (1,) * (len(extent) - position - 1))

    gain = one(*pieces[0])
    for cut in pieces[1:]:
        gain = gain * one(*cut)
    return gain


def scatter_about(rng, dims, scale, limit, split=(), kind=jnp.bfloat16):
    values = jax.random.normal(rng, dims, jnp.float32) * scale
    if len(split) > 0:
        values = level_of(rng, dims, split, -0.22, 0.18) * values
    return jnp.clip(values, min=-limit, max=limit).astype(kind)


def setup_inputs(seed: int = 0, part: int = 0) -> dict:
    seeds = jax.random.split(jax.random.key(seed), 9)
    part_splits = jax.random.split(jax.random.fold_in(seeds[8], part), 9)
    return {
        "latents": scatter_about(part_splits[0], (FRAMES, PIX, WIDTH), 1.0, 6.0, ((0, 4), (1, 4))),
        "sampled": set_ends(jax.random.randint(part_splits[1], (CLIPS,), 0, FPC), jax.random.fold_in(part_splits[1], 1), 0, FPC - 1).astype(jnp.int32),
        "temporal_gain": jnp.clip(1.0 + 0.1 * jax.random.normal(seeds[2], (WIDTH,), jnp.float32), 0.5, 1.5),
        "temporal_qkv": draw_temporal_qkv(jax.random.fold_in(seeds[8], 71), part),
        "temporal_out": scatter_about(seeds[4], (WIDTH, WIDTH), WIDTH ** -0.5, 0.3125),
        "spatial_gain": jnp.clip(1.0 + 0.1 * jax.random.normal(seeds[5], (WIDTH,), jnp.float32), 0.5, 1.5),
        "spatial_qkv": draw_spatial_qkv(jax.random.fold_in(seeds[8], 71), part),
        "spatial_out": scatter_about(seeds[7], (WIDTH, WIDTH), WIDTH ** -0.5, 0.3125),
    }


def layer_norm(frame_rows, scales):
    values = frame_rows.astype(jnp.float32)
    average = lax.optimization_barrier(jnp.mean(values, axis=-1, keepdims=True))
    centred = values - average
    spread = lax.optimization_barrier(jnp.mean(centred * centred, axis=-1, keepdims=True))
    return (centred * lax.rsqrt(spread + 1e-05) * scales).astype(jnp.bfloat16)

def project(frame_rows, matrix):
    shape = frame_rows.shape
    flat = frame_rows.reshape(-1, shape[-1])
    result = jnp.dot(flat, matrix, preferred_element_type=jnp.float32).astype(jnp.bfloat16)
    return result.reshape(shape[:-1] + (matrix.shape[1],))

def temporal_attend(queries, key_pairs, usable):
    count, pixels, channels = queries.shape
    depth = key_pairs.shape[0]
    keys = key_pairs[..., :channels].reshape(depth, pixels, HEADS, HEAD_DIM).astype(jnp.float32)
    values = key_pairs[..., channels:].reshape(depth, pixels, HEADS, HEAD_DIM).astype(jnp.float32)
    query_heads = queries.reshape(count, pixels, HEADS, HEAD_DIM).astype(jnp.float32)
    scores = jnp.einsum('fphd,kphd->phfk', query_heads, keys) / math.sqrt(HEAD_DIM)
    scores = jnp.where(usable[None, None, None, :], scores, -1e+30)
    highest = lax.optimization_barrier(jnp.max(scores, axis=-1, keepdims=True))
    expo = jnp.exp(scores - highest)
    weights = (expo / lax.optimization_barrier(jnp.sum(expo, axis=-1, keepdims=True))).astype(jnp.bfloat16)
    mixed = jnp.einsum('phfk,kphd->fphd', weights.astype(jnp.float32), values)
    return mixed.reshape(count, pixels, channels).astype(jnp.bfloat16)

def spatial_frame(frame_rows, scales, qkv_matrix, out_matrix):
    pixels, channels = frame_rows.shape
    normed = layer_norm(frame_rows, scales)
    packed = jnp.dot(normed, qkv_matrix, preferred_element_type=jnp.float32).astype(jnp.bfloat16)
    heads_view = packed.reshape(pixels, 3, HEADS, HEAD_DIM).transpose(1, 2, 0, 3)

    def one_head(triple):
        queries, keys, values = triple
        scores = jnp.dot(queries, keys.T, preferred_element_type=jnp.float32) / math.sqrt(HEAD_DIM)
        highest = lax.optimization_barrier(jnp.max(scores, axis=-1, keepdims=True))
        expo = jnp.exp(scores - highest)
        weights = (expo / lax.optimization_barrier(jnp.sum(expo, axis=-1, keepdims=True))).astype(jnp.bfloat16)
        return jnp.dot(weights, values, preferred_element_type=jnp.float32).astype(jnp.bfloat16)
    mixed = lax.map(one_head, (heads_view[0], heads_view[1], heads_view[2]))
    mixed = mixed.transpose(1, 0, 2).reshape(pixels, channels)
    update = jnp.dot(mixed, out_matrix, preferred_element_type=jnp.float32)
    return (frame_rows.astype(jnp.float32) + update).astype(jnp.bfloat16)

def reference(latents, sampled, temporal_gain, temporal_qkv, temporal_out, spatial_gain, spatial_qkv, spatial_out):
    frames, pixels, channels = latents.shape
    normed = layer_norm(latents, temporal_gain)
    queries = project(normed, temporal_qkv[:, :channels])
    key_pairs = project(normed, temporal_qkv[:, channels:])
    picks = (jnp.arange(CLIPS, dtype=jnp.int32) * FPC + sampled.astype(jnp.int32)).astype(jnp.int32)
    global_pairs = jnp.take(key_pairs, picks, axis=0)
    padded = jnp.pad(key_pairs, ((HALO, HALO), (0, 0), (0, 0)))

    def clip_step(clip_index):
        offset = (clip_index * FPC).astype(jnp.int32)
        own = lax.dynamic_slice_in_dim(queries, offset, FPC, 0)
        local = lax.dynamic_slice_in_dim(padded, offset, FPC + 2 * HALO, 0)
        positions = offset - HALO + jnp.arange(FPC + 2 * HALO, dtype=jnp.int32)
        usable = jnp.concatenate([(positions >= 0) & (positions < frames), jnp.ones((CLIPS,), jnp.bool_)])
        return temporal_attend(own, jnp.concatenate([local, global_pairs], 0), usable)
    attended = lax.map(clip_step, jnp.arange(CLIPS, dtype=jnp.int32)).reshape(frames * pixels, channels)
    update = jnp.dot(attended, temporal_out, preferred_element_type=jnp.float32)
    temporal_rows = (latents.astype(jnp.float32).reshape(-1, channels) + update).astype(jnp.bfloat16)
    temporal_rows = temporal_rows.reshape(frames, pixels, channels)
    return lax.map(lambda frame_rows: spatial_frame(frame_rows, spatial_gain, spatial_qkv, spatial_out), temporal_rows)
```

```python
import functools
import math

import jax
import jax.numpy as jnp
from jax import lax
from jax.experimental import pallas as pl
from jax.experimental.pallas import tpu as pltpu
from jax.sharding import PartitionSpec as P

HEADS = 5
HEAD_DIM = 64
HALO = 4
SUB = 8
LANES = 128
NEG = -1e30
DIRECT_CLIPS = 4
LIMIT = 24 << 20
ANY = pl.BlockSpec(memory_space=pl.ANY)
VMEM = pl.BlockSpec(memory_space=pltpu.VMEM)
NT = (((1,), (1,)), ((), ()))


def up(count, step):
    return -(-count // step) * step


def tiles_of(channels):
    return [(start, min(LANES, channels - start)) for start in range(0, channels, LANES)]


def pack(rows):
    pixels, channels = rows.shape
    parts = [rows[:, start : start + width] for start, width in tiles_of(channels) if width == LANES]
    if channels % LANES:
        tail = rows[:, channels - channels % LANES :]
        parts.append(jnp.concatenate([tail[: pixels // 2], tail[pixels // 2 :]], axis=1))
    return jnp.concatenate(parts, axis=0)


def unpack(dense, pixels, channels):
    whole = channels // LANES
    parts = [dense[i * pixels : (i + 1) * pixels] for i in range(whole)]
    if channels % LANES:
        tail = dense[whole * pixels :]
        parts.append(jnp.concatenate([tail[:, : LANES // 2], tail[:, LANES // 2 :]], axis=0))
    return jnp.concatenate(parts, axis=1)


def layer_norm(values, scales):
    average = jnp.mean(values, axis=-1, keepdims=True)
    centred = values - average
    spread = jnp.mean(centred * centred, axis=-1, keepdims=True)
    return centred * lax.rsqrt(spread + 1e-05) * scales


def own_lanes(tile, slot):
    lane = lax.broadcasted_iota(jnp.int32, tile.shape, 1)
    return (lane // HEAD_DIM) == slot


def attend(queries, keys, values, bias):
    rows, width = queries.shape
    held = width // HEAD_DIM
    if held > 1:
        zero = jnp.zeros_like(queries)
        stacked = jnp.concatenate(
            [jnp.where(own_lanes(queries, slot), queries, zero) for slot in range(held)], axis=0
        )
    else:
        stacked = queries
    scores = lax.dot_general(stacked, keys, NT, preferred_element_type=jnp.float32)
    if bias is not None:
        scores = scores + (jnp.concatenate([bias] * held, axis=0) if held > 1 else bias)
    highest = jnp.max(scores, axis=-1, keepdims=True)
    expo = jnp.exp((scores - highest) * (1.0 / math.sqrt(HEAD_DIM)))
    total = jnp.sum(expo, axis=-1, keepdims=True)
    mixed = jnp.dot(expo.astype(jnp.bfloat16), values, preferred_element_type=jnp.float32) / total
    result = mixed[:rows]
    for slot in range(1, held):
        part = mixed[slot * rows : (slot + 1) * rows]
        result = jnp.where(own_lanes(part, slot), part, result)
    return result.astype(jnp.bfloat16)


def prep_kernel(border, axis, x_hbm, s_hbm, x_ref, e_ref, o_ref, p_ref, s_ref, x_sem, s_sem):
    copy_x = pltpu.make_async_copy(x_hbm, x_ref, x_sem)
    copy_s = pltpu.make_async_copy(s_hbm, s_ref, s_sem)
    copy_x.start()
    copy_s.start()
    copy_s.wait()
    copy_x.wait()
    odd = lax.rem(lax.axis_index(axis), 2)
    frames = x_ref.shape[0]
    for i in range(border):
        e_ref[i] = pack(x_ref[(1 - odd) * (frames - border) + i])
        o_ref[i] = pack(x_ref[odd * (frames - border) + i])
    picked = pack(x_ref[s_ref[0]])
    p_ref[0] = picked
    if e_ref.shape[0] > border:
        e_ref[border] = picked
        o_ref[border] = picked


def prep(latents, sampled, with_pick):
    frames, pixels, channels = latents.shape
    dense = (pixels * channels // LANES, LANES)
    sent = HALO + (1 if with_pick else 0)
    kind = latents.dtype
    return pl.pallas_call(
        functools.partial(prep_kernel, HALO, "clip"),
        out_shape=[
            pltpu.VMEM(latents.shape, kind),
            pltpu.VMEM((sent,) + dense, kind),
            pltpu.VMEM((sent,) + dense, kind),
            pltpu.VMEM((1,) + dense, kind),
        ],
        in_specs=[ANY, ANY],
        out_specs=[VMEM] * 4,
        scratch_shapes=[
            pltpu.SMEM((1,), jnp.int32),
            pltpu.SemaphoreType.DMA,
            pltpu.SemaphoreType.DMA,
        ],
        compiler_params=pltpu.CompilerParams(vmem_limit_bytes=LIMIT),
        name="prep",
    )(latents, sampled)


def local_kernel(
    x_ref, gain_ref, tq_hbm, to_hbm, sq_hbm, so_hbm,
    q_ref, k_ref, v_ref, xg_ref, tw_ref, sw_ref, to_ref, so_ref,
    tq_ref, sq_ref, normed_ref, sems,
):
    copies = [
        pltpu.make_async_copy(source, target, sems.at[i])
        for i, (source, target) in enumerate(
            ((tq_hbm, tq_ref), (sq_hbm, sq_ref), (to_hbm, to_ref), (so_hbm, so_ref))
        )
    ]
    for copy in copies:
        copy.start()
    frames, pixels, channels = x_ref.shape
    groups = pixels // SUB
    gain = gain_ref[...]
    for f in range(frames):
        values = x_ref[f].astype(jnp.float32)
        normed = layer_norm(values, gain)
        for g in range(groups):
            xg_ref[g, f] = values[g * SUB : (g + 1) * SUB]
            normed_ref[g, f] = normed[g * SUB : (g + 1) * SUB]
    step = up(channels, LANES)

    def spread(source, target):
        target[...] = jnp.zeros_like(target)
        for part in range(3):
            target[:, part * step : part * step + channels] = source[
                :, part * channels : (part + 1) * channels
            ]

    copies[0].wait()
    spread(tq_ref, tw_ref)
    rows = normed_ref[...].reshape(groups * frames * SUB, channels).astype(jnp.bfloat16)
    packed = jnp.dot(rows, tw_ref[...], preferred_element_type=jnp.float32).astype(jnp.bfloat16)
    for part, target in enumerate((q_ref, k_ref, v_ref)):
        target[...] = packed[:, part * step : part * step + channels]
    copies[1].wait()
    spread(sq_ref, sw_ref)
    copies[2].wait()
    copies[3].wait()


def local(latents, gain, temporal_qkv, temporal_out, spatial_qkv, spatial_out):
    frames, pixels, channels = latents.shape
    count = frames * pixels
    kind = latents.dtype
    wide = (channels, 3 * up(channels, LANES))
    return pl.pallas_call(
        local_kernel,
        out_shape=[pltpu.VMEM((count, channels), kind)] * 3
        + [pltpu.VMEM((pixels // SUB, frames, SUB, channels), jnp.float32)]
        + [pltpu.VMEM(wide, kind)] * 2
        + [pltpu.VMEM((channels, channels), kind)] * 2,
        in_specs=[VMEM, pl.BlockSpec()] + [ANY] * 4,
        out_specs=[VMEM] * 8,
        scratch_shapes=[
            pltpu.VMEM(temporal_qkv.shape, kind),
            pltpu.VMEM(spatial_qkv.shape, kind),
            pltpu.VMEM((pixels // SUB, frames, SUB, channels), jnp.float32),
            pltpu.SemaphoreType.DMA((4,)),
        ],
        cost_estimate=pl.CostEstimate(
            flops=2 * count * channels * 3 * channels, bytes_accessed=4 << 20, transcendentals=0
        ),
        compiler_params=pltpu.CompilerParams(vmem_limit_bytes=LIMIT),
        name="local",
    )(latents, gain.reshape(1, channels), temporal_qkv, temporal_out, spatial_qkv, spatial_out)


def temporal_kernel(
    clips, gathered, far_steps, pix_count,
    q_ref, k_ref, v_ref, xg_ref, gain_ref, tw_ref, to_ref, e_ref, o_ref, *rest,
):
    pick_refs = rest[: 1 + (0 if gathered else len(far_steps))]
    rest = rest[len(pick_refs) :]
    sends, (normed_ref, att_ref, rows_ref) = rest[:pix_count], rest[pix_count:]
    groups, frames, _, channels = xg_ref.shape
    pixels = groups * SUB
    slots = normed_ref.shape[1]
    me = lax.axis_index("clip")
    odd = lax.rem(me, 2)
    outer = jnp.where(odd == 1, me + 1, me - 1)
    inner = jnp.where(odd == 1, me - 1, me + 1)
    outer_there = (outer >= 0) & (outer < clips)
    inner_there = inner < clips
    gain = gain_ref[...]

    dense = [e_ref[i] for i in range(HALO)] + [o_ref[i] for i in range(HALO)]
    if gathered:
        dense += [pick_refs[0][i] for i in range(clips)]
    else:
        dense += [pick_refs[0][0]]
        if clips > 1:
            dense += [e_ref[HALO]]
        for step, ref in zip(far_steps, pick_refs[1:]):
            other = jnp.bitwise_xor(me, step)
            near = jnp.abs(other - me) == 1
            dense += [jnp.where(near, o_ref[HALO], ref[0])]
    for j, frame in enumerate(dense):
        normed = layer_norm(unpack(frame, pixels, channels).astype(jnp.float32), gain)
        for g in range(groups):
            normed_ref[g, j] = normed[g * SUB : (g + 1) * SUB]
    step = up(channels, LANES)
    rows = normed_ref[...].reshape(groups * slots * SUB, channels).astype(jnp.bfloat16)
    pairs = jnp.dot(rows, tw_ref[:, step:], preferred_element_type=jnp.float32).astype(jnp.bfloat16)

    own, more = frames * SUB, slots * SUB
    shape = (own, own + more)
    row = lax.broadcasted_iota(jnp.int32, shape, 0)
    column = lax.broadcasted_iota(jnp.int32, shape, 1)
    usable = lax.rem(row, SUB) == lax.rem(column, SUB)
    slot = column // SUB - frames
    usable &= (slot < 0) | (slot >= HALO) | inner_there
    usable &= (slot < HALO) | (slot >= 2 * HALO) | outer_there
    bias = jnp.where(usable, 0.0, NEG).astype(jnp.float32)

    for g in range(groups):
        for start, width in tiles_of(channels):
            span = slice(start, start + width)
            keys = jnp.concatenate(
                [k_ref[g * own : (g + 1) * own, span], pairs[g * more : (g + 1) * more, span]], axis=0
            )
            values = jnp.concatenate(
                [
                    v_ref[g * own : (g + 1) * own, span],
                    pairs[g * more : (g + 1) * more, step + start : step + start + width],
                ],
                axis=0,
            )
            att_ref[g * own : (g + 1) * own, span] = attend(
                q_ref[g * own : (g + 1) * own, span], keys, values, bias
            )
    update = jnp.dot(att_ref[...], to_ref[...], preferred_element_type=jnp.float32)
    for g in range(groups):
        for f in range(frames):
            first = (g * frames + f) * SUB
            rows_ref[f, g * SUB : (g + 1) * SUB] = xg_ref[g, f] + update[first : first + SUB]
    place = lax.axis_index("pix")
    per_device = sends[0].shape[0]
    for k, ref in enumerate(sends):
        target = jnp.bitwise_xor(place, k)
        for i in range(per_device):
            ref[i] = pack(rows_ref[target * per_device + i].astype(jnp.bfloat16))


def temporal(parts, gain, weights, out_matrix, e, o, picks, clips, gathered, far_steps, pix_count):
    q, k, v, xg = parts
    groups, frames, _, channels = xg.shape
    pixels = groups * SUB
    slots = 2 * HALO + clips
    count = frames * pixels
    kind = q.dtype
    dense = (pixels * channels // LANES, LANES)
    return pl.pallas_call(
        functools.partial(temporal_kernel, clips, gathered, far_steps, pix_count),
        out_shape=[pltpu.VMEM((frames // pix_count,) + dense, kind)] * pix_count,
        in_specs=[VMEM] * 4 + [pl.BlockSpec()] + [VMEM] * (4 + len(picks)),
        out_specs=[VMEM] * pix_count,
        scratch_shapes=[
            pltpu.VMEM((groups, slots, SUB, channels), jnp.float32),
            pltpu.VMEM((count, channels), kind),
            pltpu.VMEM((frames, pixels, channels), jnp.float32),
        ],
        cost_estimate=pl.CostEstimate(
            flops=2 * count * channels * 4 * channels, bytes_accessed=8 << 20, transcendentals=0
        ),
        compiler_params=pltpu.CompilerParams(vmem_limit_bytes=LIMIT),
        name="temporal",
    )(q, k, v, xg, gain.reshape(1, channels), weights, out_matrix, e, o, *picks)


def spatial_kernel(pix_count, gain_ref, sw_ref, so_ref, *rest):
    chunks, out_ref, att_ref = rest[:pix_count], rest[pix_count], rest[pix_count + 1]
    per_device, pixels, channels = out_ref.shape
    each = pixels // pix_count
    step = up(channels, LANES)
    place = lax.axis_index("pix")
    gain = gain_ref[...]
    for i in range(per_device):
        rows = jnp.concatenate(
            [unpack(ref[i], each, channels) for ref in chunks], axis=0
        ).astype(jnp.float32)
        normed = layer_norm(rows, gain).astype(jnp.bfloat16)
        packed = jnp.dot(normed, sw_ref[...], preferred_element_type=jnp.float32).astype(jnp.bfloat16)
        for start, width in tiles_of(channels):
            att_ref[i, :, start : start + width] = attend(
                packed[:, start : start + width],
                packed[:, step + start : step + start + width],
                packed[:, 2 * step + start : 2 * step + start + width],
                None,
            )
        update = jnp.dot(att_ref[i], so_ref[...], preferred_element_type=jnp.float32)
        result = (rows + update).astype(jnp.bfloat16)
        for k in range(pix_count):
            first = pl.multiple_of(jnp.bitwise_xor(place, k) * each, each)
            out_ref[i, pl.ds(first, each), :] = result[k * each : (k + 1) * each]


def spatial(gain, weights, out_matrix, chunks, pixels):
    pix_count = len(chunks)
    per_device = chunks[0].shape[0]
    channels = out_matrix.shape[0]
    kind = chunks[0].dtype
    shape = (per_device, pixels, channels)
    return pl.pallas_call(
        functools.partial(spatial_kernel, pix_count),
        out_shape=jax.ShapeDtypeStruct(shape, kind),
        in_specs=[pl.BlockSpec()] + [VMEM] * (2 + pix_count),
        out_specs=pl.BlockSpec(),
        scratch_shapes=[pltpu.VMEM(shape, kind)],
        cost_estimate=pl.CostEstimate(
            flops=2 * per_device * pixels * channels * (4 * channels + 2 * pixels),
            bytes_accessed=4 << 20,
            transcendentals=0,
        ),
        compiler_params=pltpu.CompilerParams(vmem_limit_bytes=LIMIT),
        name="spatial",
    )(gain.reshape(1, channels), weights, out_matrix, *chunks)


def both_ways(pairs):
    return [pair for a, b in pairs for pair in ((a, b), (b, a))]


def body(
    latents,
    sampled,
    temporal_gain,
    temporal_qkv,
    temporal_out,
    spatial_gain,
    spatial_qkv,
    spatial_out,
):
    clips, pix_count = lax.axis_size("clip"), lax.axis_size("pix")
    pixels = latents.shape[1] * pix_count
    gathered = clips > DIRECT_CLIPS or clips & (clips - 1) != 0
    x, e, o, p = prep(latents, sampled, not gathered)
    picks, far_steps = [], ()
    if gathered:
        picks = [lax.all_gather(p, "clip", axis=0, tiled=True)]
    else:
        picks = [p]
        far_steps = tuple(range(2, clips))
        for step in far_steps:
            far = [(a, a ^ step) for a in range(clips) if (a ^ step) - a > 1]
            picks.append(lax.ppermute(p, "clip", both_ways(far)))
    e = lax.ppermute(e, "clip", both_ways([(a, a + 1) for a in range(0, clips - 1, 2)]))
    o = lax.ppermute(o, "clip", both_ways([(a, a + 1) for a in range(1, clips - 1, 2)]))
    q, k, v, xg, tw, sw, to, so = local(
        x, temporal_gain, temporal_qkv, temporal_out, spatial_qkv, spatial_out
    )
    sends = temporal(
        (q, k, v, xg), temporal_gain, tw, to, e, o, picks, clips, gathered, far_steps, pix_count
    )
    chunks = [sends[0]]
    for step in range(1, pix_count):
        chunks.append(
            lax.ppermute(sends[step], "pix", [(a, a ^ step) for a in range(pix_count)])
        )
    return spatial(spatial_gain, sw, so, chunks, pixels)


def solution(mesh):
    placed = (P(("group", "clip"), "pix", None), P(("group", "clip")), P(), P(), P(), P(), P(), P())
    return jax.shard_map(
        body,
        mesh=mesh,
        in_specs=placed,
        out_specs=P(("group", "clip", "pix"), None, None),
        check_vma=False,
    )
```

```python
import functools
import math

import jax
import jax.numpy as jnp
from jax import lax
from jax.experimental import pallas as pl
from jax.experimental.pallas import tpu as pltpu
from jax.sharding import PartitionSpec as P

HEADS = 5
HEAD_DIM = 64
HALO = 4
SUB = 8
LANES = 128
NEG = -1e30
DIRECT_CLIPS = 4
LIMIT = 24 << 20
FAR = pl.BlockSpec(memory_space=pltpu.HBM)
VMEM = pl.BlockSpec(memory_space=pltpu.VMEM)
NT = (((1,), (1,)), ((), ()))


def far(array):
    return pltpu.with_memory_space_constraint(array, pltpu.HBM)


def up(count, step):
    return -(-count // step) * step


def tiles_of(channels):
    return [(start, min(LANES, channels - start)) for start in range(0, channels, LANES)]


def pack(rows):
    pixels, channels = rows.shape
    parts = [rows[:, start : start + width] for start, width in tiles_of(channels) if width == LANES]
    if channels % LANES:
        tail = rows[:, channels - channels % LANES :]
        parts.append(jnp.concatenate([tail[: pixels // 2], tail[pixels // 2 :]], axis=1))
    return jnp.concatenate(parts, axis=0)


def unpack(dense, pixels, channels):
    whole = channels // LANES
    parts = [dense[i * pixels : (i + 1) * pixels] for i in range(whole)]
    if channels % LANES:
        tail = dense[whole * pixels :]
        parts.append(jnp.concatenate([tail[:, : LANES // 2], tail[:, LANES // 2 :]], axis=0))
    return jnp.concatenate(parts, axis=1)


def layer_norm(values, scales):
    average = jnp.mean(values, axis=-1, keepdims=True)
    centred = values - average
    spread = jnp.mean(centred * centred, axis=-1, keepdims=True)
    return centred * lax.rsqrt(spread + 1e-05) * scales


def own_lanes(tile, slot):
    lane = lax.broadcasted_iota(jnp.int32, tile.shape, 1)
    return (lane // HEAD_DIM) == slot


def attend(queries, keys, values, bias):
    rows, width = queries.shape
    held = width // HEAD_DIM
    if held > 1:
        zero = jnp.zeros_like(queries)
        stacked = jnp.concatenate(
            [jnp.where(own_lanes(queries, slot), queries, zero) for slot in range(held)], axis=0
        )
    else:
        stacked = queries
    scores = lax.dot_general(stacked, keys, NT, preferred_element_type=jnp.float32)
    if bias is not None:
        scores = scores + (jnp.concatenate([bias] * held, axis=0) if held > 1 else bias)
    highest = jnp.max(scores, axis=-1, keepdims=True)
    expo = jnp.exp((scores - highest) * (1.0 / math.sqrt(HEAD_DIM)))
    total = jnp.sum(expo, axis=-1, keepdims=True)
    mixed = jnp.dot(expo.astype(jnp.bfloat16), values, preferred_element_type=jnp.float32) / total
    result = mixed[:rows]
    for slot in range(1, held):
        part = mixed[slot * rows : (slot + 1) * rows]
        result = jnp.where(own_lanes(part, slot), part, result)
    return result.astype(jnp.bfloat16)


def prep_kernel(border, axis, x_hbm, s_ref, x_ref, e_ref, o_ref, p_ref, x_sem):
    copy_x = pltpu.make_async_copy(x_hbm, x_ref, x_sem)
    copy_x.start()
    copy_x.wait()
    odd = lax.rem(lax.axis_index(axis), 2)
    frames = x_ref.shape[0]
    for i in range(border):
        e_ref[i] = pack(x_ref[(1 - odd) * (frames - border) + i])
        o_ref[i] = pack(x_ref[odd * (frames - border) + i])
    picked = pack(x_ref[s_ref[0]])
    p_ref[0] = picked
    if e_ref.shape[0] > border:
        e_ref[border] = picked
        o_ref[border] = picked


def prep(latents, sampled, with_pick):
    frames, pixels, channels = latents.shape
    dense = (pixels * channels // LANES, LANES)
    sent = HALO + (1 if with_pick else 0)
    kind = latents.dtype
    return pl.pallas_call(
        functools.partial(prep_kernel, HALO, "clip"),
        out_shape=[
            pltpu.VMEM(latents.shape, kind),
            pltpu.VMEM((sent,) + dense, kind),
            pltpu.VMEM((sent,) + dense, kind),
            pltpu.VMEM((1,) + dense, kind),
        ],
        in_specs=[FAR, pl.BlockSpec(memory_space=pltpu.SMEM)],
        out_specs=[VMEM] * 4,
        scratch_shapes=[
            pltpu.SemaphoreType.DMA,
        ],
        compiler_params=pltpu.CompilerParams(vmem_limit_bytes=LIMIT),
        name="prep",
    )(far(latents), sampled)


def local_kernel(
    x_ref, gain_ref, tq_hbm, to_hbm, sq_hbm, so_hbm,
    q_ref, k_ref, v_ref, xg_ref, tw_ref, sw_ref, to_ref, so_ref,
    tq_ref, sq_ref, normed_ref, sems,
):
    copies = [
        pltpu.make_async_copy(source, target, sems.at[i])
        for i, (source, target) in enumerate(
            ((tq_hbm, tq_ref), (sq_hbm, sq_ref), (to_hbm, to_ref), (so_hbm, so_ref))
        )
    ]
    for copy in copies:
        copy.start()
    frames, pixels, channels = x_ref.shape
    groups = pixels // SUB
    gain = gain_ref[...]
    for f in range(frames):
        values = x_ref[f].astype(jnp.float32)
        normed = layer_norm(values, gain)
        for g in range(groups):
            xg_ref[g, f] = values[g * SUB : (g + 1) * SUB]
            normed_ref[g, f] = normed[g * SUB : (g + 1) * SUB]
    step = up(channels, LANES)

    def spread(source, target):
        target[...] = jnp.zeros_like(target)
        for part in range(3):
            target[:, part * step : part * step + channels] = source[
                :, part * channels : (part + 1) * channels
            ]

    copies[0].wait()
    spread(tq_ref, tw_ref)
    rows = normed_ref[...].reshape(groups * frames * SUB, channels).astype(jnp.bfloat16)
    packed = jnp.dot(rows, tw_ref[...], preferred_element_type=jnp.float32).astype(jnp.bfloat16)
    for part, target in enumerate((q_ref, k_ref, v_ref)):
        target[...] = packed[:, part * step : part * step + channels]
    copies[1].wait()
    spread(sq_ref, sw_ref)
    copies[2].wait()
    copies[3].wait()


def local(latents, gain, temporal_qkv, temporal_out, spatial_qkv, spatial_out):
    frames, pixels, channels = latents.shape
    count = frames * pixels
    kind = latents.dtype
    wide = (channels, 3 * up(channels, LANES))
    return pl.pallas_call(
        local_kernel,
        out_shape=[pltpu.VMEM((count, channels), kind)] * 3
        + [pltpu.VMEM((pixels // SUB, frames, SUB, channels), jnp.float32)]
        + [pltpu.VMEM(wide, kind)] * 2
        + [pltpu.VMEM((channels, channels), kind)] * 2,
        in_specs=[VMEM, pl.BlockSpec()] + [FAR] * 4,
        out_specs=[VMEM] * 8,
        scratch_shapes=[
            pltpu.VMEM(temporal_qkv.shape, kind),
            pltpu.VMEM(spatial_qkv.shape, kind),
            pltpu.VMEM((pixels // SUB, frames, SUB, channels), jnp.float32),
            pltpu.SemaphoreType.DMA((4,)),
        ],
        cost_estimate=pl.CostEstimate(
            flops=2 * count * channels * 3 * channels, bytes_accessed=4 << 20, transcendentals=0
        ),
        compiler_params=pltpu.CompilerParams(vmem_limit_bytes=LIMIT),
        name="local",
    )(
        latents,
        gain.reshape(1, channels),
        *(far(w) for w in (temporal_qkv, temporal_out, spatial_qkv, spatial_out)),
    )


def temporal_kernel(
    clips, gathered, far_steps, pix_count,
    q_ref, k_ref, v_ref, xg_ref, gain_ref, tw_ref, to_ref, e_ref, o_ref, *rest,
):
    pick_refs = rest[: 1 + (0 if gathered else len(far_steps))]
    rest = rest[len(pick_refs) :]
    sends, (normed_ref, att_ref, rows_ref) = rest[:pix_count], rest[pix_count:]
    groups, frames, _, channels = xg_ref.shape
    pixels = groups * SUB
    slots = normed_ref.shape[1]
    me = lax.axis_index("clip")
    odd = lax.rem(me, 2)
    outer = jnp.where(odd == 1, me + 1, me - 1)
    inner = jnp.where(odd == 1, me - 1, me + 1)
    outer_there = (outer >= 0) & (outer < clips)
    inner_there = inner < clips
    gain = gain_ref[...]

    dense = [e_ref[i] for i in range(HALO)] + [o_ref[i] for i in range(HALO)]
    if gathered:
        dense += [pick_refs[0][i] for i in range(clips)]
    else:
        dense += [pick_refs[0][0]]
        if clips > 1:
            dense += [e_ref[HALO]]
        for step, ref in zip(far_steps, pick_refs[1:]):
            other = jnp.bitwise_xor(me, step)
            near = jnp.abs(other - me) == 1
            dense += [jnp.where(near, o_ref[HALO], ref[0])]
    for j, frame in enumerate(dense):
        normed = layer_norm(unpack(frame, pixels, channels).astype(jnp.float32), gain)
        for g in range(groups):
            normed_ref[g, j] = normed[g * SUB : (g + 1) * SUB]
    step = up(channels, LANES)
    rows = normed_ref[...].reshape(groups * slots * SUB, channels).astype(jnp.bfloat16)
    pairs = jnp.dot(rows, tw_ref[:, step:], preferred_element_type=jnp.float32).astype(jnp.bfloat16)

    own, more = frames * SUB, slots * SUB
    shape = (own, own + more)
    row = lax.broadcasted_iota(jnp.int32, shape, 0)
    column = lax.broadcasted_iota(jnp.int32, shape, 1)
    usable = lax.rem(row, SUB) == lax.rem(column, SUB)
    slot = column // SUB - frames
    usable &= (slot < 0) | (slot >= HALO) | inner_there
    usable &= (slot < HALO) | (slot >= 2 * HALO) | outer_there
    bias = jnp.where(usable, 0.0, NEG).astype(jnp.float32)

    for g in range(groups):
        for start, width in tiles_of(channels):
            span = slice(start, start + width)
            keys = jnp.concatenate(
                [k_ref[g * own : (g + 1) * own, span], pairs[g * more : (g + 1) * more, span]], axis=0
            )
            values = jnp.concatenate(
                [
                    v_ref[g * own : (g + 1) * own, span],
                    pairs[g * more : (g + 1) * more, step + start : step + start + width],
                ],
                axis=0,
            )
            att_ref[g * own : (g + 1) * own, span] = attend(
                q_ref[g * own : (g + 1) * own, span], keys, values, bias
            )
    update = jnp.dot(att_ref[...], to_ref[...], preferred_element_type=jnp.float32)
    for g in range(groups):
        for f in range(frames):
            first = (g * frames + f) * SUB
            rows_ref[f, g * SUB : (g + 1) * SUB] = xg_ref[g, f] + update[first : first + SUB]
    place = lax.axis_index("pix")
    per_device = sends[0].shape[0]
    for k, ref in enumerate(sends):
        target = jnp.bitwise_xor(place, k)
        for i in range(per_device):
            ref[i] = pack(rows_ref[target * per_device + i].astype(jnp.bfloat16))


def temporal(parts, gain, weights, out_matrix, e, o, picks, clips, gathered, far_steps, pix_count):
    q, k, v, xg = parts
    groups, frames, _, channels = xg.shape
    pixels = groups * SUB
    slots = 2 * HALO + clips
    count = frames * pixels
    kind = q.dtype
    dense = (pixels * channels // LANES, LANES)
    return pl.pallas_call(
        functools.partial(temporal_kernel, clips, gathered, far_steps, pix_count),
        out_shape=[pltpu.VMEM((frames // pix_count,) + dense, kind)] * pix_count,
        in_specs=[VMEM] * 4 + [pl.BlockSpec()] + [VMEM] * (4 + len(picks)),
        out_specs=[VMEM] * pix_count,
        scratch_shapes=[
            pltpu.VMEM((groups, slots, SUB, channels), jnp.float32),
            pltpu.VMEM((count, channels), kind),
            pltpu.VMEM((frames, pixels, channels), jnp.float32),
        ],
        cost_estimate=pl.CostEstimate(
            flops=2 * count * channels * 4 * channels, bytes_accessed=8 << 20, transcendentals=0
        ),
        compiler_params=pltpu.CompilerParams(vmem_limit_bytes=LIMIT),
        name="temporal",
    )(q, k, v, xg, gain.reshape(1, channels), weights, out_matrix, e, o, *picks)


def spatial_kernel(pix_count, gain_ref, sw_ref, so_ref, *rest):
    chunks, out_ref, att_ref = rest[:pix_count], rest[pix_count], rest[pix_count + 1]
    per_device, pixels, channels = out_ref.shape
    each = pixels // pix_count
    step = up(channels, LANES)
    place = lax.axis_index("pix")
    gain = gain_ref[...]
    for i in range(per_device):
        rows = jnp.concatenate(
            [unpack(ref[i], each, channels) for ref in chunks], axis=0
        ).astype(jnp.float32)
        normed = layer_norm(rows, gain).astype(jnp.bfloat16)
        packed = jnp.dot(normed, sw_ref[...], preferred_element_type=jnp.float32).astype(jnp.bfloat16)
        for start, width in tiles_of(channels):
            att_ref[i, :, start : start + width] = attend(
                packed[:, start : start + width],
                packed[:, step + start : step + start + width],
                packed[:, 2 * step + start : 2 * step + start + width],
                None,
            )
        update = jnp.dot(att_ref[i], so_ref[...], preferred_element_type=jnp.float32)
        result = (rows + update).astype(jnp.bfloat16)
        for k in range(pix_count):
            first = pl.multiple_of(jnp.bitwise_xor(place, k) * each, each)
            out_ref[i, pl.ds(first, each), :] = result[k * each : (k + 1) * each]


def spatial(gain, weights, out_matrix, chunks, pixels):
    pix_count = len(chunks)
    per_device = chunks[0].shape[0]
    channels = out_matrix.shape[0]
    kind = chunks[0].dtype
    shape = (per_device, pixels, channels)
    return pl.pallas_call(
        functools.partial(spatial_kernel, pix_count),
        out_shape=jax.ShapeDtypeStruct(shape, kind),
        in_specs=[pl.BlockSpec()] + [VMEM] * (2 + pix_count),
        out_specs=pl.BlockSpec(),
        scratch_shapes=[pltpu.VMEM(shape, kind)],
        cost_estimate=pl.CostEstimate(
            flops=2 * per_device * pixels * channels * (4 * channels + 2 * pixels),
            bytes_accessed=4 << 20,
            transcendentals=0,
        ),
        compiler_params=pltpu.CompilerParams(vmem_limit_bytes=LIMIT),
        name="spatial",
    )(gain.reshape(1, channels), weights, out_matrix, *chunks)


def both_ways(pairs):
    return [pair for a, b in pairs for pair in ((a, b), (b, a))]


def body(
    latents,
    sampled,
    temporal_gain,
    temporal_qkv,
    temporal_out,
    spatial_gain,
    spatial_qkv,
    spatial_out,
):
    clips, pix_count = lax.axis_size("clip"), lax.axis_size("pix")
    pixels = latents.shape[1] * pix_count
    gathered = clips > DIRECT_CLIPS or clips & (clips - 1) != 0
    x, e, o, p = prep(latents, sampled, not gathered)
    picks, far_steps = [], ()
    if gathered:
        picks = [lax.all_gather(p, "clip", axis=0, tiled=True)]
    else:
        picks = [p]
        far_steps = tuple(range(2, clips))
        for step in far_steps:
            distant = [(a, a ^ step) for a in range(clips) if (a ^ step) - a > 1]
            picks.append(lax.ppermute(p, "clip", both_ways(distant)))
    e = lax.ppermute(e, "clip", both_ways([(a, a + 1) for a in range(0, clips - 1, 2)]))
    o = lax.ppermute(o, "clip", both_ways([(a, a + 1) for a in range(1, clips - 1, 2)]))
    q, k, v, xg, tw, sw, to, so = local(
        x, temporal_gain, temporal_qkv, temporal_out, spatial_qkv, spatial_out
    )
    sends = temporal(
        (q, k, v, xg), temporal_gain, tw, to, e, o, picks, clips, gathered, far_steps, pix_count
    )
    chunks = [sends[0]]
    for step in range(1, pix_count):
        chunks.append(
            lax.ppermute(sends[step], "pix", [(a, a ^ step) for a in range(pix_count)])
        )
    return spatial(spatial_gain, sw, so, chunks, pixels)


def solution(mesh):
    placed = (P(("group", "clip"), "pix", None), P(("group", "clip")), P(), P(), P(), P(), P(), P())
    return jax.shard_map(
        body,
        mesh=mesh,
        in_specs=placed,
        out_specs=P(("group", "clip", "pix"), None, None),
        check_vma=False,
    )
```

```python
import functools
import math

import jax
import jax.numpy as jnp
from jax import lax
from jax.experimental import pallas as pl
from jax.experimental.pallas import tpu as pltpu
from jax.sharding import PartitionSpec as P

HEAD_DIM = 64
HALO = 4
SUB = 8
LANES = 128
NEG = -1e30
DIRECT_CLIPS = 4
LIMIT = 24 << 20
LEAD = 1
FAR = pl.BlockSpec(memory_space=pltpu.HBM)
VMEM = pl.BlockSpec(memory_space=pltpu.VMEM)
NT = (((1,), (1,)), ((), ()))


def far(array):
    return pltpu.with_memory_space_constraint(array, pltpu.HBM)


def up(count, step):
    return -(-count // step) * step


def tiles_of(channels):
    return [(start, min(LANES, channels - start)) for start in range(0, channels, LANES)]


def pack(rows):
    pixels, channels = rows.shape
    parts = [rows[:, start : start + width] for start, width in tiles_of(channels) if width == LANES]
    if channels % LANES:
        tail = rows[:, channels - channels % LANES :]
        parts.append(jnp.concatenate([tail[: pixels // 2], tail[pixels // 2 :]], axis=1))
    return jnp.concatenate(parts, axis=0)


def unpack(dense, pixels, channels):
    whole = channels // LANES
    parts = [dense[i * pixels : (i + 1) * pixels] for i in range(whole)]
    if channels % LANES:
        tail = dense[whole * pixels :]
        parts.append(jnp.concatenate([tail[:, : LANES // 2], tail[:, LANES // 2 :]], axis=0))
    return jnp.concatenate(parts, axis=1)


def layer_norm(values, scales):
    share = 1.0 / values.shape[-1]
    average = jnp.sum(values, axis=-1, keepdims=True) * share
    centred = values - average
    spread = jnp.sum(centred * centred, axis=-1, keepdims=True) * share
    return centred * lax.rsqrt(spread + 1e-05) * scales


def own_lanes(shape, slot):
    return (lax.broadcasted_iota(jnp.int32, shape, 1) // HEAD_DIM) == slot


def stack_heads(queries):
    held = queries.shape[1] // HEAD_DIM
    if held == 1:
        return queries
    zero = jnp.zeros_like(queries)
    return jnp.concatenate(
        [jnp.where(own_lanes(queries.shape, slot), queries, zero) for slot in range(held)], axis=0
    )


def unstack_heads(mixed, held):
    rows = mixed.shape[0] // held
    result = mixed[:rows]
    for slot in range(1, held):
        part = mixed[slot * rows : (slot + 1) * rows]
        result = jnp.where(own_lanes(part.shape, slot), part, result)
    return result


def soften(scores):
    highest = jnp.max(scores, axis=-1, keepdims=True)
    expo = jnp.exp((scores - highest) * (1.0 / math.sqrt(HEAD_DIM)))
    return expo.astype(jnp.bfloat16), 1.0 / jnp.sum(expo, axis=-1, keepdims=True)


def pipelined(count, score, mix, lead=1):
    scores, weights = {}, {}
    for i in range(count + 2 * lead):
        if i < count:
            scores[i] = score(i)
        if 0 <= i - lead < count:
            weights[i - lead] = soften(scores.pop(i - lead))
        if 0 <= i - 2 * lead < count:
            mix(i - 2 * lead, *weights.pop(i - 2 * lead))


def neighbours(clips):
    me = lax.axis_index("clip")
    odd = lax.rem(me, 2)
    outer = jnp.where(odd == 1, me + 1, me - 1)
    inner = jnp.where(odd == 1, me - 1, me + 1)
    outer_there = (outer >= 0) & (outer < clips)
    inner_there = inner < clips
    return me, odd, inner_there, outer_there


def prep_kernel(clips, x_hbm, s_ref, x_ref, a_ref, b_ref, p_ref, x_sem):
    copy_x = pltpu.make_async_copy(x_hbm, x_ref, x_sem)
    copy_x.start()
    _, odd, _, _ = neighbours(clips)
    copy_x.wait()
    span = x_ref.shape[0] - HALO
    for i in range(HALO):
        a_ref[i] = pack(x_ref[(1 - odd) * span + i])
        b_ref[i] = pack(x_ref[odd * span + i])
    picked = pack(x_ref[s_ref[0]])
    p_ref[0] = picked
    if a_ref.shape[0] > HALO:
        a_ref[HALO] = picked
        b_ref[HALO] = picked


def prep(latents, sampled, clips, with_pick):
    _, pixels, channels = latents.shape
    dense = (pixels * channels // LANES, LANES)
    sent = HALO + (1 if with_pick else 0)
    kind = latents.dtype
    return pl.pallas_call(
        functools.partial(prep_kernel, clips),
        out_shape=[
            pltpu.VMEM(latents.shape, kind),
            pltpu.VMEM((sent,) + dense, kind),
            pltpu.VMEM((sent,) + dense, kind),
            pltpu.VMEM((1,) + dense, kind),
        ],
        in_specs=[FAR, pl.BlockSpec(memory_space=pltpu.SMEM)],
        out_specs=[VMEM] * 4,
        scratch_shapes=[pltpu.SemaphoreType.DMA],
        compiler_params=pltpu.CompilerParams(vmem_limit_bytes=LIMIT),
        name="prep",
    )(far(latents), sampled)


def local_kernel(
    x_ref, gain_ref, tq_hbm, to_hbm, sq_hbm, so_hbm,
    q_ref, k_ref, v_ref, xg_ref, tw_ref, sw_ref, to_ref, so_ref,
    tq_ref, sq_ref, sp_ref, normed_ref, sems,
):
    copies = [
        pltpu.make_async_copy(source, target, sems.at[i])
        for i, (source, target) in enumerate(
            ((tq_hbm, tq_ref), (sq_hbm, sq_ref), (to_hbm, to_ref), (so_hbm, sp_ref))
        )
    ]
    for copy in copies:
        copy.start()
    frames, pixels, channels = x_ref.shape
    groups = pixels // SUB
    gain = gain_ref[...]
    for f in range(frames):
        values = x_ref[f].astype(jnp.float32)
        normed = layer_norm(values, gain)
        for g in range(groups):
            xg_ref[g, f] = values[g * SUB : (g + 1) * SUB]
            normed_ref[g, f] = normed[g * SUB : (g + 1) * SUB]
    step = up(channels, LANES)

    def spread(source, target):
        for part in range(3):
            target[:, part * step : part * step + channels] = source[
                :, part * channels : (part + 1) * channels
            ]
            if step > channels:
                target[:, part * step + channels : (part + 1) * step] = jnp.zeros(
                    (channels, step - channels), target.dtype
                )

    copies[0].wait()
    spread(tq_ref, tw_ref)
    rows = normed_ref[...].reshape(groups * frames * SUB, channels).astype(jnp.bfloat16)
    packed = jnp.dot(rows, tw_ref[...], preferred_element_type=jnp.float32).astype(jnp.bfloat16)
    own = frames * SUB
    for g in range(groups):
        for start, width in tiles_of(channels):
            stacked = stack_heads(packed[g * own : (g + 1) * own, start : start + width])
            q_ref[g, start // HEAD_DIM * own : start // HEAD_DIM * own + stacked.shape[0], :width] = stacked
    k_ref[...] = packed[:, step : step + channels]
    v_ref[...] = packed[:, 2 * step : 2 * step + channels]
    copies[1].wait()
    spread(sq_ref, sw_ref)
    copies[2].wait()
    copies[3].wait()
    so_ref[...] = sp_ref[...].T


def local(latents, gain, temporal_qkv, temporal_out, spatial_qkv, spatial_out):
    frames, pixels, channels = latents.shape
    groups = pixels // SUB
    count = frames * pixels
    kind = latents.dtype
    wide = (channels, 3 * up(channels, LANES))
    square = (channels, channels)
    return pl.pallas_call(
        local_kernel,
        out_shape=[pltpu.VMEM((groups, channels // HEAD_DIM * frames * SUB, LANES), kind)]
        + [pltpu.VMEM((count, channels), kind)] * 2
        + [pltpu.VMEM((groups, frames, SUB, channels), jnp.float32)]
        + [pltpu.VMEM(wide, kind)] * 2
        + [pltpu.VMEM(square, kind)] * 2,
        in_specs=[VMEM, pl.BlockSpec()] + [FAR] * 4,
        out_specs=[VMEM] * 8,
        scratch_shapes=[
            pltpu.VMEM(temporal_qkv.shape, kind),
            pltpu.VMEM(spatial_qkv.shape, kind),
            pltpu.VMEM(square, kind),
            pltpu.VMEM((groups, frames, SUB, channels), jnp.float32),
            pltpu.SemaphoreType.DMA((4,)),
        ],
        cost_estimate=pl.CostEstimate(
            flops=2 * count * channels * 3 * channels, bytes_accessed=4 << 20, transcendentals=0
        ),
        compiler_params=pltpu.CompilerParams(vmem_limit_bytes=LIMIT),
        name="local",
    )(
        latents,
        gain.reshape(1, channels),
        *(far(w) for w in (temporal_qkv, temporal_out, spatial_qkv, spatial_out)),
    )


def remote_pairs(dense, gain, tw_ref, normed_ref, pixels):
    channels = gain.shape[1]
    groups, slots = normed_ref.shape[:2]
    for j, frame in enumerate(dense):
        normed = layer_norm(unpack(frame, pixels, channels).astype(jnp.float32), gain)
        for g in range(groups):
            normed_ref[g, j] = normed[g * SUB : (g + 1) * SUB]
    for j in range(len(dense), slots):
        for g in range(groups):
            normed_ref[g, j] = jnp.zeros((SUB, channels), jnp.float32)
    step = up(channels, LANES)
    rows = normed_ref[...].reshape(groups * slots * SUB, channels).astype(jnp.bfloat16)
    return jnp.dot(rows, tw_ref[:, step:], preferred_element_type=jnp.float32).astype(jnp.bfloat16)


def early_kernel(gain_ref, tw_ref, a_ref, *rest):
    *pick_refs, kv_ref, normed_ref = rest
    dense = [a_ref[i] for i in range(a_ref.shape[0])]
    for ref in pick_refs:
        dense += [ref[i] for i in range(ref.shape[0])]
    pixels = normed_ref.shape[0] * SUB
    kv_ref[...] = remote_pairs(dense, gain_ref[...], tw_ref, normed_ref, pixels)


def early(gain, weights, a, picks, pixels, slots):
    channels = weights.shape[0]
    groups = pixels // SUB
    kind = weights.dtype
    return pl.pallas_call(
        early_kernel,
        out_shape=pltpu.VMEM((pixels * slots, 2 * up(channels, LANES)), kind),
        in_specs=[pl.BlockSpec()] + [VMEM] * (2 + len(picks)),
        out_specs=VMEM,
        scratch_shapes=[pltpu.VMEM((groups, slots, SUB, channels), jnp.float32)],
        cost_estimate=pl.CostEstimate(
            flops=2 * pixels * slots * channels * 2 * channels, bytes_accessed=2 << 20, transcendentals=0
        ),
        compiler_params=pltpu.CompilerParams(vmem_limit_bytes=LIMIT),
        name="early",
    )(gain.reshape(1, channels), weights, a, *picks)


def temporal_kernel(
    clips, far_steps, early_held, pix_count,
    q_ref, k_ref, v_ref, xg_ref, kv_ref, gain_ref, tw_ref, to_ref, b_ref, *rest,
):
    sends, (normed_ref, att_ref, rows_ref) = rest[:pix_count], rest[pix_count:]
    groups, frames, _, channels = xg_ref.shape
    pixels = groups * SUB
    me, _, first_there, second_there = neighbours(clips)
    held = b_ref.shape[0]
    dense = [b_ref[i] for i in range(held)]
    late = remote_pairs(dense, gain_ref[...], tw_ref, normed_ref, pixels)
    step = up(channels, LANES)

    own, soon, more = frames * SUB, kv_ref.shape[0] // groups, late.shape[0] // groups
    shape = (own, own + soon + more)
    row = lax.broadcasted_iota(jnp.int32, shape, 0)
    column = lax.broadcasted_iota(jnp.int32, shape, 1)
    usable = lax.rem(row, SUB) == lax.rem(column, SUB)
    slot = column // SUB - frames
    usable &= (slot < 0) | (slot >= held) | first_there
    usable &= (slot < early_held) | (slot >= soon // SUB)
    for i, hop in enumerate(far_steps):
        distant = jnp.abs(jnp.bitwise_xor(me, hop) - me) > 1
        usable &= (slot != held + 1 + i) | distant
    usable &= (slot < soon // SUB) | (slot >= soon // SUB + held) | second_there
    usable &= slot < soon // SUB + held
    bias = jnp.where(usable, 0.0, NEG).astype(jnp.float32)

    tiles = tiles_of(channels)
    blocks = [(g, start, width) for g in range(groups) for start, width in tiles]

    def score(i):
        g, start, width = blocks[i]
        span = slice(start, start + width)
        count = width // HEAD_DIM
        queries = q_ref[g, start // HEAD_DIM * own : (start + width) // HEAD_DIM * own, :width]
        keys = jnp.concatenate(
            [
                k_ref[g * own : (g + 1) * own, span],
                kv_ref[g * soon : (g + 1) * soon, span],
                late[g * more : (g + 1) * more, span],
            ],
            axis=0,
        )
        scores = lax.dot_general(queries, keys, NT, preferred_element_type=jnp.float32)
        return scores + jnp.concatenate([bias] * count, axis=0)

    def mix(i, weights, norm):
        g, start, width = blocks[i]
        values = jnp.concatenate(
            [
                v_ref[g * own : (g + 1) * own, start : start + width],
                kv_ref[g * soon : (g + 1) * soon, step + start : step + start + width],
                late[g * more : (g + 1) * more, step + start : step + start + width],
            ],
            axis=0,
        )
        mixed = jnp.dot(weights, values, preferred_element_type=jnp.float32) * norm
        att_ref[g * own : (g + 1) * own, start : start + width] = unstack_heads(
            mixed, width // HEAD_DIM
        ).astype(jnp.bfloat16)

    pipelined(len(blocks), score, mix, LEAD)
    update = jnp.dot(att_ref[...], to_ref[...], preferred_element_type=jnp.float32)
    for g in range(groups):
        for f in range(frames):
            at = (g * frames + f) * SUB
            rows_ref[f, g * SUB : (g + 1) * SUB] = xg_ref[g, f] + update[at : at + SUB]
    place = lax.axis_index("pix")
    per_device = sends[0].shape[0]
    for k, ref in enumerate(sends):
        target = jnp.bitwise_xor(place, k)
        for i in range(per_device):
            ref[i] = pack(rows_ref[target * per_device + i].astype(jnp.bfloat16))


def temporal(parts, pairs, gain, weights, out_matrix, b, clips, far_steps, early_held, pix_count):
    q, k, v, xg = parts
    groups, frames, _, channels = xg.shape
    pixels = groups * SUB
    slots = up(b.shape[0], 2)
    count = frames * pixels
    kind = q.dtype
    dense = (pixels * channels // LANES, LANES)
    return pl.pallas_call(
        functools.partial(temporal_kernel, clips, far_steps, early_held, pix_count),
        out_shape=[pltpu.VMEM((frames // pix_count,) + dense, kind)] * pix_count,
        in_specs=[VMEM] * 5 + [pl.BlockSpec()] + [VMEM] * 3,
        out_specs=[VMEM] * pix_count,
        scratch_shapes=[
            pltpu.VMEM((groups, slots, SUB, channels), jnp.float32),
            pltpu.VMEM((count, channels), kind),
            pltpu.VMEM((frames, pixels, channels), jnp.float32),
        ],
        cost_estimate=pl.CostEstimate(
            flops=2 * count * channels * 4 * channels, bytes_accessed=8 << 20, transcendentals=0
        ),
        compiler_params=pltpu.CompilerParams(vmem_limit_bytes=LIMIT),
        name="temporal",
    )(q, k, v, xg, pairs, gain.reshape(1, channels), weights, out_matrix, b)


def spatial_kernel(pix_count, gain_ref, sw_ref, so_ref, *rest):
    chunks, (out_ref, rows_ref, att_ref) = rest[:pix_count], rest[pix_count:]
    per_device, channels, pixels = out_ref.shape
    each = pixels // pix_count
    step = up(channels, LANES)
    place = lax.axis_index("pix")
    for k, ref in enumerate(chunks):
        at = pl.multiple_of(jnp.bitwise_xor(place, k) * each, each)
        for i in range(per_device):
            rows_ref[i, pl.ds(at, each), :] = unpack(ref[i], each, channels).astype(jnp.float32)
    rows = rows_ref[...].reshape(per_device * pixels, channels)
    normed = layer_norm(rows, gain_ref[...]).astype(jnp.bfloat16)
    packed = jnp.dot(normed, sw_ref[...], preferred_element_type=jnp.float32).astype(jnp.bfloat16)
    tiles = tiles_of(channels)
    blocks = [(i, start, width) for i in range(per_device) for start, width in tiles]

    def part_of(i, which):
        frame, start, width = blocks[i]
        return packed[
            frame * pixels : (frame + 1) * pixels, which * step + start : which * step + start + width
        ]

    def score(i):
        return lax.dot_general(
            stack_heads(part_of(i, 0)), part_of(i, 1), NT, preferred_element_type=jnp.float32
        )

    def mix(i, weights, norm):
        frame, start, width = blocks[i]
        mixed = jnp.dot(weights, part_of(i, 2), preferred_element_type=jnp.float32) * norm
        att_ref[frame, :, start : start + width] = unstack_heads(mixed, width // HEAD_DIM).astype(
            jnp.bfloat16
        )

    pipelined(len(blocks), score, mix)
    for i in range(per_device):
        update = lax.dot_general(so_ref[...], att_ref[i], NT, preferred_element_type=jnp.float32)
        out_ref[i] = (rows_ref[i].T + update).astype(jnp.bfloat16)


def spatial(gain, weights, out_matrix, chunks, pixels):
    pix_count = len(chunks)
    per_device = chunks[0].shape[0]
    channels = out_matrix.shape[0]
    kind = chunks[0].dtype
    return pl.pallas_call(
        functools.partial(spatial_kernel, pix_count),
        out_shape=jax.ShapeDtypeStruct((per_device, channels, pixels), kind),
        in_specs=[pl.BlockSpec()] + [VMEM] * (2 + pix_count),
        out_specs=pl.BlockSpec(),
        scratch_shapes=[
            pltpu.VMEM((per_device, pixels, channels), jnp.float32),
            pltpu.VMEM((per_device, pixels, channels), kind),
        ],
        cost_estimate=pl.CostEstimate(
            flops=2 * per_device * pixels * channels * (4 * channels + 2 * pixels),
            bytes_accessed=4 << 20,
            transcendentals=0,
        ),
        compiler_params=pltpu.CompilerParams(vmem_limit_bytes=LIMIT),
        name="spatial",
    )(gain.reshape(1, channels), weights, out_matrix, *chunks)


def both_ways(pairs, count):
    target = [device ^ 1 for device in range(count)]
    for a, b in pairs:
        target[a], target[b] = b, a
    return list(enumerate(target))


def border_pairs(clips, pix_count, turn):
    pairs = [
        (a * pix_count + place, (a + 1) * pix_count + place)
        for a in range(turn, clips - 1, 2)
        for place in range(pix_count)
    ]
    return both_ways(pairs, clips * pix_count)


def body(
    latents,
    sampled,
    temporal_gain,
    temporal_qkv,
    temporal_out,
    spatial_gain,
    spatial_qkv,
    spatial_out,
):
    clips, pix_count = lax.axis_size("clip"), lax.axis_size("pix")
    pixels = latents.shape[1] * pix_count
    gathered = clips > DIRECT_CLIPS or clips & (clips - 1) != 0
    x, a, b, p = prep(latents, sampled, clips, not gathered)
    far_steps = ()
    if gathered:
        picks = [lax.all_gather(p, "clip", axis=0, tiled=True)]
    else:
        picks = [p]
        far_steps = tuple(range(2, clips))
        for step in far_steps:
            distant = [
                (i * pix_count + place, (i ^ step) * pix_count + place)
                for i in range(clips)
                if (i ^ step) - i > 1
                for place in range(pix_count)
            ]
            picks.append(lax.ppermute(p, ("clip", "pix"), both_ways(distant, clips * pix_count)))
    a = lax.ppermute(a, ("clip", "pix"), border_pairs(clips, pix_count, 0))
    b = lax.ppermute(b, ("clip", "pix"), border_pairs(clips, pix_count, 1))
    q, k, v, xg, tw, sw, to, so = local(
        x, temporal_gain, temporal_qkv, temporal_out, spatial_qkv, spatial_out
    )
    early_held = a.shape[0] + sum(pick.shape[0] for pick in picks)
    pairs = early(temporal_gain, tw, a, picks, latents.shape[1], up(early_held, 2))
    sends = temporal(
        (q, k, v, xg), pairs, temporal_gain, tw, to, b, clips, far_steps, early_held, pix_count
    )
    chunks = [sends[0]]
    for step in range(1, pix_count):
        chunks.append(lax.ppermute(sends[step], "pix", [(i, i ^ step) for i in range(pix_count)]))
    return spatial(spatial_gain, sw, so, chunks, pixels).transpose(0, 2, 1)


def solution(mesh):
    placed = (P(("group", "clip"), "pix", None), P(("group", "clip")), P(), P(), P(), P(), P(), P())
    return jax.shard_map(
        body,
        mesh=mesh,
        in_specs=placed,
        out_specs=P(("group", "clip", "pix"), None, None),
        check_vma=False,
    )
```

```python
import functools
import math

import jax
import jax.numpy as jnp
from jax import lax
from jax.experimental import pallas as pl
from jax.experimental.pallas import tpu as pltpu
from jax.sharding import PartitionSpec as P

HEAD_DIM = 64
HALO = 4
SUB = 8
LANES = 128
NEG = -1e30
DIRECT_CLIPS = 4
LIMIT = 24 << 20
LEAD = 4
SPATIAL_LEAD = 2
FAR = pl.BlockSpec(memory_space=pltpu.HBM)
VMEM = pl.BlockSpec(memory_space=pltpu.VMEM)
NT = (((1,), (1,)), ((), ()))


def far(array):
    return pltpu.with_memory_space_constraint(array, pltpu.HBM)


def up(count, step):
    return -(-count // step) * step


def tiles_of(channels):
    return [(start, min(LANES, channels - start)) for start in range(0, channels, LANES)]


def pack(rows):
    pixels, channels = rows.shape
    parts = [rows[:, start : start + width] for start, width in tiles_of(channels) if width == LANES]
    if channels % LANES:
        tail = rows[:, channels - channels % LANES :]
        parts.append(jnp.concatenate([tail[: pixels // 2], tail[pixels // 2 :]], axis=1))
    return jnp.concatenate(parts, axis=0)


def unpack(dense, pixels, channels):
    whole = channels // LANES
    parts = [dense[i * pixels : (i + 1) * pixels] for i in range(whole)]
    if channels % LANES:
        tail = dense[whole * pixels :]
        parts.append(jnp.concatenate([tail[:, : LANES // 2], tail[:, LANES // 2 :]], axis=0))
    return jnp.concatenate(parts, axis=1)


def layer_norm(values, scales):
    share = 1.0 / values.shape[-1]
    average = jnp.sum(values, axis=-1, keepdims=True) * share
    centred = values - average
    spread = jnp.sum(centred * centred, axis=-1, keepdims=True) * share
    return centred * lax.rsqrt(spread + 1e-05) * scales


def own_lanes(shape, slot):
    return (lax.broadcasted_iota(jnp.int32, shape, 1) // HEAD_DIM) == slot


def stack_heads(queries):
    held = queries.shape[1] // HEAD_DIM
    if held == 1:
        return queries
    zero = jnp.zeros_like(queries)
    return jnp.concatenate(
        [jnp.where(own_lanes(queries.shape, slot), queries, zero) for slot in range(held)], axis=0
    )


def unstack_heads(mixed, held):
    rows = mixed.shape[0] // held
    result = mixed[:rows]
    for slot in range(1, held):
        part = mixed[slot * rows : (slot + 1) * rows]
        result = jnp.where(own_lanes(part.shape, slot), part, result)
    return result


def soften(scores):
    highest = jnp.max(scores, axis=-1, keepdims=True)
    expo = jnp.exp((scores - highest) * (1.0 / math.sqrt(HEAD_DIM)))
    return expo.astype(jnp.bfloat16), 1.0 / jnp.sum(expo, axis=-1, keepdims=True)


def pipelined(count, score, mix, lead=1):
    scores, weights = {}, {}
    for i in range(count + 2 * lead):
        if i < count:
            scores[i] = score(i)
        if 0 <= i - lead < count:
            weights[i - lead] = soften(scores.pop(i - lead))
        if 0 <= i - 2 * lead < count:
            mix(i - 2 * lead, *weights.pop(i - 2 * lead))


def neighbours(clips):
    me = lax.axis_index("clip")
    odd = lax.rem(me, 2)
    outer = jnp.where(odd == 1, me + 1, me - 1)
    inner = jnp.where(odd == 1, me - 1, me + 1)
    outer_there = (outer >= 0) & (outer < clips)
    inner_there = inner < clips
    return me, odd, inner_there, outer_there


def prep_kernel(clips, x_hbm, s_ref, x_ref, a_ref, b_ref, p_ref, x_sem):
    copy_x = pltpu.make_async_copy(x_hbm, x_ref, x_sem)
    copy_x.start()
    _, odd, _, _ = neighbours(clips)
    copy_x.wait()
    span = x_ref.shape[0] - HALO
    for i in range(HALO):
        a_ref[i] = pack(x_ref[(1 - odd) * span + i])
        b_ref[i] = pack(x_ref[odd * span + i])
    picked = pack(x_ref[s_ref[0]])
    p_ref[0] = picked
    if a_ref.shape[0] > HALO:
        a_ref[HALO] = picked


def prep(latents, sampled, clips, with_pick):
    _, pixels, channels = latents.shape
    dense = (pixels * channels // LANES, LANES)
    sent = HALO + (1 if with_pick else 0)
    kind = latents.dtype
    return pl.pallas_call(
        functools.partial(prep_kernel, clips),
        out_shape=[
            pltpu.VMEM(latents.shape, kind),
            pltpu.VMEM((sent,) + dense, kind),
            pltpu.VMEM((HALO,) + dense, kind),
            pltpu.VMEM((1,) + dense, kind),
        ],
        in_specs=[FAR, pl.BlockSpec(memory_space=pltpu.SMEM)],
        out_specs=[VMEM] * 4,
        scratch_shapes=[pltpu.SemaphoreType.DMA],
        compiler_params=pltpu.CompilerParams(vmem_limit_bytes=LIMIT),
        name="prep",
    )(far(latents), sampled)


def local_kernel(
    x_ref, gain_ref, tq_hbm, to_hbm, sq_hbm, so_hbm,
    q_ref, k_ref, v_ref, xg_ref, tw_ref, sw_ref, to_ref, so_ref,
    tq_ref, sq_ref, sp_ref, normed_ref, sems,
):
    copies = [
        pltpu.make_async_copy(source, target, sems.at[i])
        for i, (source, target) in enumerate(
            ((tq_hbm, tq_ref), (sq_hbm, sq_ref), (to_hbm, to_ref), (so_hbm, sp_ref))
        )
    ]
    for copy in copies:
        copy.start()
    frames, pixels, channels = x_ref.shape
    groups = pixels // SUB
    gain = gain_ref[...]
    for f in range(frames):
        values = x_ref[f].astype(jnp.float32)
        normed = layer_norm(values, gain)
        for g in range(groups):
            xg_ref[g, f] = values[g * SUB : (g + 1) * SUB]
            normed_ref[g, f] = normed[g * SUB : (g + 1) * SUB]
    step = up(channels, LANES)

    def spread(source, target):
        for part in range(3):
            target[:, part * step : part * step + channels] = source[
                :, part * channels : (part + 1) * channels
            ]
            if step > channels:
                target[:, part * step + channels : (part + 1) * step] = jnp.zeros(
                    (channels, step - channels), target.dtype
                )

    copies[0].wait()
    spread(tq_ref, tw_ref)
    rows = normed_ref[...].reshape(groups * frames * SUB, channels).astype(jnp.bfloat16)
    packed = jnp.dot(rows, tw_ref[...], preferred_element_type=jnp.float32).astype(jnp.bfloat16)
    own = frames * SUB
    for g in range(groups):
        for start, width in tiles_of(channels):
            for half in range(2):
                at = g * own + half * (own // 2)
                stacked = stack_heads(packed[at : at + own // 2, start : start + width])
                first = start // HEAD_DIM * (own // 2)
                q_ref[g, half, first : first + stacked.shape[0], :width] = stacked
    k_ref[...] = packed[:, step : step + channels]
    v_ref[...] = packed[:, 2 * step : 2 * step + channels]
    copies[1].wait()
    spread(sq_ref, sw_ref)
    copies[2].wait()
    copies[3].wait()
    so_ref[...] = sp_ref[...].T


def local(latents, gain, temporal_qkv, temporal_out, spatial_qkv, spatial_out):
    frames, pixels, channels = latents.shape
    groups = pixels // SUB
    count = frames * pixels
    kind = latents.dtype
    wide = (channels, 3 * up(channels, LANES))
    square = (channels, channels)
    return pl.pallas_call(
        local_kernel,
        out_shape=[pltpu.VMEM((groups, 2, channels // HEAD_DIM * frames * SUB // 2, LANES), kind)]
        + [pltpu.VMEM((count, channels), kind)] * 2
        + [pltpu.VMEM((groups, frames, SUB, channels), jnp.float32)]
        + [pltpu.VMEM(wide, kind)] * 2
        + [pltpu.VMEM(square, kind)] * 2,
        in_specs=[VMEM, pl.BlockSpec()] + [FAR] * 4,
        out_specs=[VMEM] * 8,
        scratch_shapes=[
            pltpu.VMEM(temporal_qkv.shape, kind),
            pltpu.VMEM(spatial_qkv.shape, kind),
            pltpu.VMEM(square, kind),
            pltpu.VMEM((groups, frames, SUB, channels), jnp.float32),
            pltpu.SemaphoreType.DMA((4,)),
        ],
        cost_estimate=pl.CostEstimate(
            flops=2 * count * channels * 3 * channels, bytes_accessed=4 << 20, transcendentals=0
        ),
        compiler_params=pltpu.CompilerParams(vmem_limit_bytes=LIMIT),
        name="local",
    )(
        latents,
        gain.reshape(1, channels),
        *(far(w) for w in (temporal_qkv, temporal_out, spatial_qkv, spatial_out)),
    )


def remote_pairs(dense, gain, tw_ref, normed_ref, pixels):
    channels = gain.shape[1]
    groups, slots = normed_ref.shape[:2]
    for j, frame in enumerate(dense):
        normed = layer_norm(unpack(frame, pixels, channels).astype(jnp.float32), gain)
        for g in range(groups):
            normed_ref[g, j] = normed[g * SUB : (g + 1) * SUB]
    for j in range(len(dense), slots):
        for g in range(groups):
            normed_ref[g, j] = jnp.zeros((SUB, channels), jnp.float32)
    step = up(channels, LANES)
    rows = normed_ref[...].reshape(groups * slots * SUB, channels).astype(jnp.bfloat16)
    return jnp.dot(rows, tw_ref[:, step:], preferred_element_type=jnp.float32).astype(jnp.bfloat16)


def early_kernel(gain_ref, tw_ref, a_ref, *rest):
    *pick_refs, kv_ref, normed_ref = rest
    dense = [a_ref[i] for i in range(a_ref.shape[0])]
    for ref in pick_refs:
        dense += [ref[i] for i in range(ref.shape[0])]
    pixels = normed_ref.shape[0] * SUB
    kv_ref[...] = remote_pairs(dense, gain_ref[...], tw_ref, normed_ref, pixels)


def early(gain, weights, a, picks, pixels, slots):
    channels = weights.shape[0]
    groups = pixels // SUB
    kind = weights.dtype
    return pl.pallas_call(
        early_kernel,
        out_shape=pltpu.VMEM((pixels * slots, 2 * up(channels, LANES)), kind),
        in_specs=[pl.BlockSpec()] + [VMEM] * (2 + len(picks)),
        out_specs=VMEM,
        scratch_shapes=[pltpu.VMEM((groups, slots, SUB, channels), jnp.float32)],
        cost_estimate=pl.CostEstimate(
            flops=2 * pixels * slots * channels * 2 * channels, bytes_accessed=2 << 20, transcendentals=0
        ),
        compiler_params=pltpu.CompilerParams(vmem_limit_bytes=LIMIT),
        name="early",
    )(gain.reshape(1, channels), weights, a, *picks)


def temporal_kernel(
    clips, early_held, pix_count, cross,
    q_ref, k_ref, v_ref, xg_ref, kv_ref, gain_ref, tw_ref, to_ref, b_ref, *rest,
):
    halves = pix_count // 2
    sends, rest = rest[:halves], rest[halves:]
    groups, frames, _, channels = xg_ref.shape
    pixels = groups * SUB
    _, _, first_there, second_there = neighbours(clips)
    if cross:
        late_ref, normed_ref, att_ref, rows_ref = rest
        dense = [b_ref[i] for i in range(HALO)]
        late_ref[...] = remote_pairs(dense, gain_ref[...], tw_ref, normed_ref, pixels)
    else:
        late_ref = b_ref
        att_ref, rows_ref = rest
    place = lax.axis_index("pix")
    upper = place // halves
    half = 1 - upper if cross else upper
    step = up(channels, LANES)

    part = frames // 2
    mine, own = part * SUB, frames * SUB
    soon, more = kv_ref.shape[0] // groups, late_ref.shape[0] // groups
    shape = (mine, own + soon + more)
    row = lax.broadcasted_iota(jnp.int32, shape, 0)
    column = lax.broadcasted_iota(jnp.int32, shape, 1)
    usable = lax.rem(row, SUB) == lax.rem(column, SUB)
    slot = column // SUB - frames
    usable &= (slot < 0) | (slot >= HALO) | first_there
    usable &= (slot < early_held) | (slot >= soon // SUB)
    usable &= (slot < soon // SUB) | second_there
    bias = jnp.where(usable, 0.0, NEG).astype(jnp.float32)

    blocks = [(g, start, width) for g in range(groups) for start, width in tiles_of(channels)]

    def score(i):
        g, start, width = blocks[i]
        span = slice(start, start + width)
        queries = q_ref[
            g, half, start // HEAD_DIM * mine : (start + width) // HEAD_DIM * mine, :width
        ]
        keys = jnp.concatenate(
            [
                k_ref[g * own : (g + 1) * own, span],
                kv_ref[g * soon : (g + 1) * soon, span],
                late_ref[g * more : (g + 1) * more, span],
            ],
            axis=0,
        )
        scores = lax.dot_general(queries, keys, NT, preferred_element_type=jnp.float32)
        return scores + jnp.concatenate([bias] * (width // HEAD_DIM), axis=0)

    def mix(i, weights, norm):
        g, start, width = blocks[i]
        values = jnp.concatenate(
            [
                v_ref[g * own : (g + 1) * own, start : start + width],
                kv_ref[g * soon : (g + 1) * soon, step + start : step + start + width],
                late_ref[g * more : (g + 1) * more, step + start : step + start + width],
            ],
            axis=0,
        )
        mixed = jnp.dot(weights, values, preferred_element_type=jnp.float32) * norm
        att_ref[g * mine : (g + 1) * mine, start : start + width] = unstack_heads(
            mixed, width // HEAD_DIM
        ).astype(jnp.bfloat16)

    pipelined(len(blocks), score, mix, LEAD)
    update = jnp.dot(att_ref[...], to_ref[...], preferred_element_type=jnp.float32)
    for g in range(groups):
        for f in range(part):
            at = (g * part + f) * SUB
            rows_ref[f, g * SUB : (g + 1) * SUB] = xg_ref[g, half * part + f] + update[at : at + SUB]
    per_device = sends[0].shape[0]
    for k, ref in enumerate(sends):
        target = jnp.bitwise_xor(lax.rem(place, halves), k)
        for i in range(per_device):
            ref[i] = pack(rows_ref[target * per_device + i].astype(jnp.bfloat16))


def temporal(parts, pairs, gain, weights, out_matrix, last, clips, early_held, pix_count, cross):
    q, k, v, xg = parts
    groups, frames, _, channels = xg.shape
    pixels = groups * SUB
    count = frames * pixels
    kind = q.dtype
    dense = (pixels * channels // LANES, LANES)
    out_shape = [pltpu.VMEM((frames // pix_count,) + dense, kind)] * (pix_count // 2)
    scratch = [
        pltpu.VMEM((count // 2, channels), kind),
        pltpu.VMEM((frames // 2, pixels, channels), jnp.float32),
    ]
    if cross:
        out_shape = out_shape + [pltpu.VMEM((pixels * HALO, 2 * up(channels, LANES)), kind)]
        scratch = [pltpu.VMEM((groups, HALO, SUB, channels), jnp.float32)] + scratch
    return pl.pallas_call(
        functools.partial(temporal_kernel, clips, early_held, pix_count, cross),
        out_shape=out_shape,
        in_specs=[VMEM] * 5 + [pl.BlockSpec()] + [VMEM] * 3,
        out_specs=[VMEM] * len(out_shape),
        scratch_shapes=scratch,
        cost_estimate=pl.CostEstimate(
            flops=2 * count * channels * 2 * channels, bytes_accessed=4 << 20, transcendentals=0
        ),
        compiler_params=pltpu.CompilerParams(vmem_limit_bytes=LIMIT),
        name="cross" if cross else "near",
    )(q, k, v, xg, pairs, gain.reshape(1, channels), weights, out_matrix, last)


def gather_rows(chunks, rows_ref, channels):
    halves = len(chunks)
    per_device, half_pixels = rows_ref.shape[:2]
    each = half_pixels // halves
    place = lax.rem(lax.axis_index("pix"), halves)
    for k, ref in enumerate(chunks):
        at = pl.multiple_of(jnp.bitwise_xor(place, k) * each, each)
        for i in range(per_device):
            rows_ref[i, pl.ds(at, each), :] = unpack(ref[i], each, channels).astype(jnp.float32)
    return rows_ref[...].reshape(per_device * half_pixels, channels)


def project_half(rows, gain, sw_ref):
    normed = layer_norm(rows, gain).astype(jnp.bfloat16)
    return jnp.dot(normed, sw_ref[...], preferred_element_type=jnp.float32).astype(jnp.bfloat16)


def ready_kernel(halves, gain_ref, sw_ref, *rest):
    chunks, (packed_ref, flipped_ref, rows_ref) = rest[:halves], rest[halves:]
    channels = sw_ref.shape[0]
    rows = gather_rows(chunks, rows_ref, channels)
    packed_ref[...] = project_half(rows, gain_ref[...], sw_ref)
    for i in range(rows_ref.shape[0]):
        flipped_ref[i] = rows_ref[i].T


def ready(gain, weights, chunks, pixels):
    halves = len(chunks)
    per_device = chunks[0].shape[0]
    channels = weights.shape[0]
    kind = chunks[0].dtype
    half = pixels // 2
    return pl.pallas_call(
        functools.partial(ready_kernel, halves),
        out_shape=[
            pltpu.VMEM((per_device * half, weights.shape[1]), kind),
            pltpu.VMEM((per_device, channels, half), jnp.float32),
        ],
        in_specs=[pl.BlockSpec()] + [VMEM] * (1 + halves),
        out_specs=[VMEM] * 2,
        scratch_shapes=[pltpu.VMEM((per_device, half, channels), jnp.float32)],
        cost_estimate=pl.CostEstimate(
            flops=2 * per_device * half * channels * 3 * channels,
            bytes_accessed=2 << 20,
            transcendentals=0,
        ),
        compiler_params=pltpu.CompilerParams(vmem_limit_bytes=LIMIT),
        name="ready",
    )(gain.reshape(1, channels), weights, *chunks)


def spatial_kernel(halves, gain_ref, sw_ref, so_ref, packed_ref, flipped_ref, *rest):
    chunks, (out_ref, rows_ref, att_ref) = rest[:halves], rest[halves:]
    per_device, channels, pixels = out_ref.shape
    half = pixels // 2
    step = up(channels, LANES)
    rows = gather_rows(chunks, rows_ref, channels)
    late = project_half(rows, gain_ref[...], sw_ref)
    blocks = [
        (i, start, width, side)
        for i in range(per_device)
        for start, width in tiles_of(channels)
        for side in range(2)
    ]

    def part_of(frame, which, start, width, side):
        at = which * step + start
        source = late if side else packed_ref
        return source[frame * half : (frame + 1) * half, at : at + width]

    def both(frame, which, start, width):
        return jnp.concatenate(
            [part_of(frame, which, start, width, side) for side in range(2)], axis=0
        )

    def score(i):
        frame, start, width, side = blocks[i]
        return lax.dot_general(
            stack_heads(part_of(frame, 0, start, width, side)),
            both(frame, 1, start, width),
            NT,
            preferred_element_type=jnp.float32,
        )

    def mix(i, weights, norm):
        frame, start, width, side = blocks[i]
        mixed = jnp.dot(weights, both(frame, 2, start, width), preferred_element_type=jnp.float32) * norm
        att_ref[frame, side * half : (side + 1) * half, start : start + width] = unstack_heads(
            mixed, width // HEAD_DIM
        ).astype(jnp.bfloat16)

    pipelined(len(blocks), score, mix, SPATIAL_LEAD)
    upper = lax.axis_index("pix") // halves
    for i in range(per_device):
        update = lax.dot_general(so_ref[...], att_ref[i], NT, preferred_element_type=jnp.float32)
        here = pl.multiple_of(upper * half, half)
        there = pl.multiple_of((1 - upper) * half, half)
        out_ref[i, :, pl.ds(here, half)] = (flipped_ref[i] + update[:, :half]).astype(jnp.bfloat16)
        out_ref[i, :, pl.ds(there, half)] = (rows_ref[i].T + update[:, half:]).astype(jnp.bfloat16)


def spatial(gain, weights, out_matrix, packed, flipped, chunks, pixels):
    halves = len(chunks)
    per_device = chunks[0].shape[0]
    channels = out_matrix.shape[0]
    kind = chunks[0].dtype
    return pl.pallas_call(
        functools.partial(spatial_kernel, halves),
        out_shape=jax.ShapeDtypeStruct((per_device, channels, pixels), kind),
        in_specs=[pl.BlockSpec()] + [VMEM] * (4 + halves),
        out_specs=pl.BlockSpec(),
        scratch_shapes=[
            pltpu.VMEM((per_device, pixels // 2, channels), jnp.float32),
            pltpu.VMEM((per_device, pixels, channels), kind),
        ],
        cost_estimate=pl.CostEstimate(
            flops=2 * per_device * pixels * channels * (4 * channels + 2 * pixels),
            bytes_accessed=4 << 20,
            transcendentals=0,
        ),
        compiler_params=pltpu.CompilerParams(vmem_limit_bytes=LIMIT),
        name="spatial",
    )(gain.reshape(1, channels), weights, out_matrix, packed, flipped, *chunks)


def both_ways(pairs, count):
    target = [device ^ 1 for device in range(count)]
    for a, b in pairs:
        target[a], target[b] = b, a
    return list(enumerate(target))


def border_pairs(clips, pix_count, turn):
    pairs = [
        (a * pix_count + place, (a + 1) * pix_count + place)
        for a in range(turn, clips - 1, 2)
        for place in range(pix_count)
    ]
    return both_ways(pairs, clips * pix_count)


def body(
    latents,
    sampled,
    temporal_gain,
    temporal_qkv,
    temporal_out,
    spatial_gain,
    spatial_qkv,
    spatial_out,
):
    clips, pix_count = lax.axis_size("clip"), lax.axis_size("pix")
    pixels = latents.shape[1] * pix_count
    gathered = clips > DIRECT_CLIPS or clips & (clips - 1) != 0
    x, a, b, p = prep(latents, sampled, clips, not gathered)
    if gathered:
        picks = [lax.all_gather(p, "clip", axis=0, tiled=True)]
    else:
        picks = [p]
        for step in range(2, clips):
            picks.append(lax.ppermute(p, "clip", [(i, i ^ step) for i in range(clips)]))
    a = lax.ppermute(a, ("clip", "pix"), border_pairs(clips, pix_count, 0))
    b = lax.ppermute(b, ("clip", "pix"), border_pairs(clips, pix_count, 1))
    q, k, v, xg, tw, sw, to, so = local(
        x, temporal_gain, temporal_qkv, temporal_out, spatial_qkv, spatial_out
    )
    early_held = a.shape[0] + sum(pick.shape[0] for pick in picks)
    pairs = early(temporal_gain, tw, a, picks, latents.shape[1], up(early_held, 2))
    rest = ((q, k, v, xg), pairs, temporal_gain, tw, to)
    halves = pix_count // 2
    *sends, late = temporal(*rest, b, clips, early_held, pix_count, True)

    def swap(chunk, step):
        return lax.ppermute(chunk, "pix", [(i, i ^ step) for i in range(pix_count)])

    crossed = [swap(sends[k], halves + k) for k in range(halves)]
    kept = temporal(*rest, late, clips, early_held, pix_count, False)
    held = [kept[0]] + [swap(kept[k], k) for k in range(1, halves)]
    packed, flipped = ready(spatial_gain, sw, held, pixels)
    return spatial(spatial_gain, sw, so, packed, flipped, crossed, pixels).transpose(0, 2, 1)


def solution(mesh):
    placed = (P(("group", "clip"), "pix", None), P(("group", "clip")), P(), P(), P(), P(), P(), P())
    return jax.shard_map(
        body,
        mesh=mesh,
        in_specs=placed,
        out_specs=P(("group", "clip", "pix"), None, None),
        check_vma=False,
    )
```

```python
import functools
import math

import jax
import jax.numpy as jnp
from jax import lax
from jax.experimental import pallas as pl
from jax.experimental.pallas import tpu as pltpu
from jax.sharding import PartitionSpec as P

HEAD_DIM = 64
HALO = 4
SUB = 8
LANES = 128
NEG = -1e30
DIRECT_CLIPS = 4
LIMIT = 24 << 20
LEAD = 8
SPATIAL_LEAD = 2
SIDES = ((0, 1),)
FAR = pl.BlockSpec(memory_space=pltpu.HBM)
VMEM = pl.BlockSpec(memory_space=pltpu.VMEM)
NT = (((1,), (1,)), ((), ()))


def far(array):
    return pltpu.with_memory_space_constraint(array, pltpu.HBM)


def up(count, step):
    return -(-count // step) * step


def tiles_of(channels):
    return [(start, min(LANES, channels - start)) for start in range(0, channels, LANES)]


class Tile:
    def __init__(self, query, key, value, start, width):
        self.query, self.key, self.value = query, key, value
        self.start, self.width = start, width
        self.held, self.head = width // HEAD_DIM, start // HEAD_DIM


def plan(channels):
    whole = channels // LANES * LANES
    tiles = [
        Tile(start, whole + start, 2 * whole + start, start, LANES) for start in range(0, whole, LANES)
    ]
    if channels > whole:
        tiles.append(Tile(3 * whole, 3 * whole + LANES, 3 * whole, whole, channels - whole))
    return tiles


def planned_width(channels):
    whole = channels // LANES * LANES
    return 3 * whole + (2 * LANES if channels > whole else 0)


def pack(rows):
    pixels, channels = rows.shape
    parts = [rows[:, start : start + width] for start, width in tiles_of(channels) if width == LANES]
    if channels % LANES:
        tail = rows[:, channels - channels % LANES :]
        parts.append(jnp.concatenate([tail[: pixels // 2], tail[pixels // 2 :]], axis=1))
    return jnp.concatenate(parts, axis=0)


def unpack(dense, pixels, channels):
    whole = channels // LANES
    parts = [dense[i * pixels : (i + 1) * pixels] for i in range(whole)]
    if channels % LANES:
        tail = dense[whole * pixels :]
        parts.append(jnp.concatenate([tail[:, : LANES // 2], tail[:, LANES // 2 :]], axis=0))
    return jnp.concatenate(parts, axis=1)


def layer_norm(values, scales):
    share = 1.0 / values.shape[-1]
    average = jnp.sum(values, axis=-1, keepdims=True) * share
    centred = values - average
    spread = jnp.sum(centred * centred, axis=-1, keepdims=True) * share
    return centred * lax.rsqrt(spread + 1e-05) * scales


def own_lanes(shape, slot):
    return (lax.broadcasted_iota(jnp.int32, shape, 1) // HEAD_DIM) == slot


def stack_heads(queries, held):
    if held == 1:
        return queries
    zero = jnp.zeros_like(queries)
    return jnp.concatenate(
        [jnp.where(own_lanes(queries.shape, slot), queries, zero) for slot in range(held)], axis=0
    )


def unstack_heads(mixed, held):
    rows = mixed.shape[0] // held
    result = mixed[:rows]
    for slot in range(1, held):
        part = mixed[slot * rows : (slot + 1) * rows]
        result = jnp.where(own_lanes(part.shape, slot), part, result)
    return result


def soften(scores):
    highest = jnp.max(scores, axis=-1, keepdims=True)
    expo = jnp.exp((scores - highest) * (1.0 / math.sqrt(HEAD_DIM)))
    return expo.astype(jnp.bfloat16), 1.0 / jnp.sum(expo, axis=-1, keepdims=True)


def pipelined(count, score, mix, lead=1):
    scores, weights = {}, {}
    for i in range(count + 2 * lead):
        if i < count:
            scores[i] = score(i)
        if 0 <= i - lead < count:
            weights[i - lead] = soften(scores.pop(i - lead))
        if 0 <= i - 2 * lead < count:
            mix(i - 2 * lead, *weights.pop(i - 2 * lead))


def neighbours(clips):
    me = lax.axis_index("clip")
    odd = lax.rem(me, 2)
    outer = jnp.where(odd == 1, me + 1, me - 1)
    inner = jnp.where(odd == 1, me - 1, me + 1)
    outer_there = (outer >= 0) & (outer < clips)
    inner_there = inner < clips
    return me, odd, inner_there, outer_there


def prep_kernel(clips, x_hbm, s_ref, x_ref, a_ref, b_ref, p_ref, x_sem):
    copy_x = pltpu.make_async_copy(x_hbm, x_ref, x_sem)
    copy_x.start()
    _, odd, _, _ = neighbours(clips)
    copy_x.wait()
    span = x_ref.shape[0] - HALO
    for i in range(HALO):
        a_ref[i] = pack(x_ref[(1 - odd) * span + i])
        b_ref[i] = pack(x_ref[odd * span + i])
    picked = pack(x_ref[s_ref[0]])
    p_ref[0] = picked
    if a_ref.shape[0] > HALO:
        a_ref[HALO] = picked


def prep(latents, sampled, clips, with_pick):
    _, pixels, channels = latents.shape
    dense = (pixels * channels // LANES, LANES)
    sent = HALO + (1 if with_pick else 0)
    kind = latents.dtype
    return pl.pallas_call(
        functools.partial(prep_kernel, clips),
        out_shape=[
            pltpu.VMEM(latents.shape, kind),
            pltpu.VMEM((sent,) + dense, kind),
            pltpu.VMEM((HALO,) + dense, kind),
            pltpu.VMEM((1,) + dense, kind),
        ],
        in_specs=[FAR, pl.BlockSpec(memory_space=pltpu.SMEM)],
        out_specs=[VMEM] * 4,
        scratch_shapes=[pltpu.SemaphoreType.DMA],
        compiler_params=pltpu.CompilerParams(vmem_limit_bytes=LIMIT),
        name="prep",
    )(far(latents), sampled)


def local_kernel(
    x_ref, gain_ref, tq_hbm, to_hbm, sq_hbm, so_hbm,
    q_ref, kv_ref, xg_ref, tw_ref, sw_ref, to_ref, so_ref,
    tq_ref, sq_ref, sp_ref, normed_ref, sems,
):
    copies = [
        pltpu.make_async_copy(source, target, sems.at[i])
        for i, (source, target) in enumerate(
            ((tq_hbm, tq_ref), (sq_hbm, sq_ref), (to_hbm, to_ref), (so_hbm, sp_ref))
        )
    ]
    for copy in copies:
        copy.start()
    frames, pixels, channels = x_ref.shape
    groups = pixels // SUB
    gain = gain_ref[...]
    for f in range(frames):
        values = x_ref[f].astype(jnp.float32)
        normed = layer_norm(values, gain)
        for g in range(groups):
            xg_ref[g, f] = values[g * SUB : (g + 1) * SUB]
            normed_ref[g, f] = normed[g * SUB : (g + 1) * SUB]
    whole = channels // LANES * LANES

    def spread(source, target):
        parts = [source[:, i * channels : (i + 1) * channels] for i in range(3)]
        for i, part in enumerate(parts):
            target[:, i * whole : (i + 1) * whole] = part[:, :whole]
        if channels > whole:
            queries, keys, values = (part[:, whole:] for part in parts)
            tail = jnp.concatenate([values, queries], axis=1)
            target[:, 3 * whole : 3 * whole + LANES] = tail
            target[:, 3 * whole + LANES :] = jnp.concatenate([jnp.zeros_like(keys), keys], axis=1)

    copies[0].wait()
    spread(tq_ref, tw_ref)
    rows = normed_ref[...].reshape(groups * frames * SUB, channels).astype(jnp.bfloat16)
    packed = jnp.dot(rows, tw_ref[...], preferred_element_type=jnp.float32).astype(jnp.bfloat16)
    own = frames * SUB
    for g in range(groups):
        for tile in plan(channels):
            for half in range(2):
                at = g * own + half * (own // 2)
                stacked = stack_heads(
                    packed[at : at + own // 2, tile.query : tile.query + LANES], tile.held
                )
                first = tile.head * (own // 2)
                q_ref[g, half, first : first + stacked.shape[0], :] = stacked
    kv_ref[...] = packed[:, whole:]
    copies[1].wait()
    spread(sq_ref, sw_ref)
    copies[2].wait()
    copies[3].wait()
    so_ref[...] = sp_ref[...].T


def local(latents, gain, temporal_qkv, temporal_out, spatial_qkv, spatial_out):
    frames, pixels, channels = latents.shape
    groups = pixels // SUB
    count = frames * pixels
    kind = latents.dtype
    wide = (channels, planned_width(channels))
    square = (channels, channels)
    pair_width = wide[1] - channels // LANES * LANES
    return pl.pallas_call(
        local_kernel,
        out_shape=[pltpu.VMEM((groups, 2, channels // HEAD_DIM * frames * SUB // 2, LANES), kind)]
        + [pltpu.VMEM((count, pair_width), kind)]
        + [pltpu.VMEM((groups, frames, SUB, channels), jnp.float32)]
        + [pltpu.VMEM(wide, kind)] * 2
        + [pltpu.VMEM(square, kind)] * 2,
        in_specs=[VMEM, pl.BlockSpec()] + [FAR] * 4,
        out_specs=[VMEM] * 7,
        scratch_shapes=[
            pltpu.VMEM(temporal_qkv.shape, kind),
            pltpu.VMEM(spatial_qkv.shape, kind),
            pltpu.VMEM(square, kind),
            pltpu.VMEM((groups, frames, SUB, channels), jnp.float32),
            pltpu.SemaphoreType.DMA((4,)),
        ],
        cost_estimate=pl.CostEstimate(
            flops=2 * count * channels * 3 * channels, bytes_accessed=4 << 20, transcendentals=0
        ),
        compiler_params=pltpu.CompilerParams(vmem_limit_bytes=LIMIT),
        name="local",
    )(
        latents,
        gain.reshape(1, channels),
        *(far(w) for w in (temporal_qkv, temporal_out, spatial_qkv, spatial_out)),
    )


def remote_pairs(dense, gain, tw_ref, normed_ref, pixels):
    channels = gain.shape[1]
    groups, slots = normed_ref.shape[:2]
    for j, frame in enumerate(dense):
        normed = layer_norm(unpack(frame, pixels, channels).astype(jnp.float32), gain)
        for g in range(groups):
            normed_ref[g, j] = normed[g * SUB : (g + 1) * SUB]
    for j in range(len(dense), slots):
        for g in range(groups):
            normed_ref[g, j] = jnp.zeros((SUB, channels), jnp.float32)
    whole = channels // LANES * LANES
    rows = normed_ref[...].reshape(groups * slots * SUB, channels).astype(jnp.bfloat16)
    return jnp.dot(rows, tw_ref[:, whole:], preferred_element_type=jnp.float32).astype(jnp.bfloat16)


def early_kernel(gain_ref, tw_ref, a_ref, *rest):
    *pick_refs, kv_ref, normed_ref = rest
    dense = [a_ref[i] for i in range(a_ref.shape[0])]
    for ref in pick_refs:
        dense += [ref[i] for i in range(ref.shape[0])]
    pixels = normed_ref.shape[0] * SUB
    kv_ref[...] = remote_pairs(dense, gain_ref[...], tw_ref, normed_ref, pixels)


def early(gain, weights, a, picks, pixels, slots):
    channels = weights.shape[0]
    groups = pixels // SUB
    kind = weights.dtype
    return pl.pallas_call(
        early_kernel,
        out_shape=pltpu.VMEM((pixels * slots, weights.shape[1] - channels // LANES * LANES), kind),
        in_specs=[pl.BlockSpec()] + [VMEM] * (2 + len(picks)),
        out_specs=VMEM,
        scratch_shapes=[pltpu.VMEM((groups, slots, SUB, channels), jnp.float32)],
        cost_estimate=pl.CostEstimate(
            flops=2 * pixels * slots * channels * 2 * channels, bytes_accessed=2 << 20, transcendentals=0
        ),
        compiler_params=pltpu.CompilerParams(vmem_limit_bytes=LIMIT),
        name="early",
    )(gain.reshape(1, channels), weights, a, *picks)


def temporal_kernel(
    clips, early_held, late_held, pix_count, cross,
    q_ref, own_ref, xg_ref, kv_ref, gain_ref, tw_ref, to_ref, *rest,
):
    halves = pix_count // 2
    scratch = 4 if cross else 2
    last_refs, sends, rest = (
        rest[: len(rest) - halves - scratch],
        rest[len(rest) - halves - scratch : len(rest) - scratch],
        rest[len(rest) - scratch :],
    )
    groups, frames, _, channels = xg_ref.shape
    pixels = groups * SUB
    _, _, first_there, second_there = neighbours(clips)
    if cross:
        late_ref, normed_ref, att_ref, rows_ref = rest
        dense = [ref[i] for ref in last_refs for i in range(ref.shape[0])]
        late_ref[...] = remote_pairs(dense, gain_ref[...], tw_ref, normed_ref, pixels)
    else:
        (late_ref,) = last_refs
        att_ref, rows_ref = rest
    place = lax.axis_index("pix")
    upper = place // halves
    half = 1 - upper if cross else upper
    whole = channels // LANES * LANES

    part = frames // 2
    mine, own = part * SUB, frames * SUB
    soon, more = kv_ref.shape[0] // groups, late_ref.shape[0] // groups
    shape = (mine, own + soon + more)
    row = lax.broadcasted_iota(jnp.int32, shape, 0)
    column = lax.broadcasted_iota(jnp.int32, shape, 1)
    usable = lax.rem(row, SUB) == lax.rem(column, SUB)
    slot = column // SUB - frames
    usable &= (slot < 0) | (slot >= HALO) | first_there
    usable &= (slot < early_held) | (slot >= soon // SUB)
    usable &= (slot < soon // SUB) | (slot >= soon // SUB + HALO) | second_there
    usable &= slot < soon // SUB + late_held
    bias = jnp.where(usable, 0.0, NEG).astype(jnp.float32)

    blocks = [(g, tile) for g in range(groups) for tile in plan(channels)]

    def pairs_of(g, column):
        span = slice(column - whole, column - whole + LANES)
        return jnp.concatenate(
            [
                own_ref[g * own : (g + 1) * own, span],
                kv_ref[g * soon : (g + 1) * soon, span],
                late_ref[g * more : (g + 1) * more, span],
            ],
            axis=0,
        )

    def score(i):
        g, tile = blocks[i]
        queries = q_ref[g, half, tile.head * mine : (tile.head + tile.held) * mine, :]
        scores = lax.dot_general(
            queries, pairs_of(g, tile.key), NT, preferred_element_type=jnp.float32
        )
        return scores + jnp.concatenate([bias] * tile.held, axis=0)

    def mix(i, weights, norm):
        g, tile = blocks[i]
        mixed = jnp.dot(weights, pairs_of(g, tile.value), preferred_element_type=jnp.float32) * norm
        att_ref[g * mine : (g + 1) * mine, tile.start : tile.start + tile.width] = unstack_heads(
            mixed, tile.held
        )[:, : tile.width].astype(jnp.bfloat16)

    pipelined(len(blocks), score, mix, LEAD)
    update = jnp.dot(att_ref[...], to_ref[...], preferred_element_type=jnp.float32)
    for g in range(groups):
        for f in range(part):
            at = (g * part + f) * SUB
            rows_ref[f, g * SUB : (g + 1) * SUB] = xg_ref[g, half * part + f] + update[at : at + SUB]
    per_device = sends[0].shape[0]
    for k, ref in enumerate(sends):
        target = jnp.bitwise_xor(lax.rem(place, halves), k)
        for i in range(per_device):
            ref[i] = pack(rows_ref[target * per_device + i].astype(jnp.bfloat16))


def temporal(
    parts, pairs, gain, weights, out_matrix, last, clips, early_held, late_held, pix_count, cross
):
    q, own, xg = parts
    groups, frames, _, channels = xg.shape
    pixels = groups * SUB
    count = frames * pixels
    kind = q.dtype
    dense = (pixels * channels // LANES, LANES)
    out_shape = [pltpu.VMEM((frames // pix_count,) + dense, kind)] * (pix_count // 2)
    scratch = [
        pltpu.VMEM((count // 2, channels), kind),
        pltpu.VMEM((frames // 2, pixels, channels), jnp.float32),
    ]
    if cross:
        slots = up(late_held, 2)
        out_shape = out_shape + [pltpu.VMEM((pixels * slots, pairs.shape[1]), kind)]
        scratch = [pltpu.VMEM((groups, slots, SUB, channels), jnp.float32)] + scratch
    return pl.pallas_call(
        functools.partial(temporal_kernel, clips, early_held, late_held, pix_count, cross),
        out_shape=out_shape,
        in_specs=[VMEM] * 4 + [pl.BlockSpec()] + [VMEM] * (2 + len(last)),
        out_specs=[VMEM] * len(out_shape),
        scratch_shapes=scratch,
        cost_estimate=pl.CostEstimate(
            flops=2 * count * channels * 2 * channels, bytes_accessed=4 << 20, transcendentals=0
        ),
        compiler_params=pltpu.CompilerParams(vmem_limit_bytes=LIMIT),
        name="cross" if cross else "near",
    )(q, own, xg, pairs, gain.reshape(1, channels), weights, out_matrix, *last)


def gather_rows(chunks, rows_ref, channels):
    halves = len(chunks)
    per_device, half_pixels = rows_ref.shape[:2]
    each = half_pixels // halves
    place = lax.rem(lax.axis_index("pix"), halves)
    for k, ref in enumerate(chunks):
        at = pl.multiple_of(jnp.bitwise_xor(place, k) * each, each)
        for i in range(per_device):
            rows_ref[i, pl.ds(at, each), :] = unpack(ref[i], each, channels).astype(jnp.float32)
    return rows_ref[...].reshape(per_device * half_pixels, channels)


def project_half(rows, gain, sw_ref):
    normed = layer_norm(rows, gain).astype(jnp.bfloat16)
    return jnp.dot(normed, sw_ref[...], preferred_element_type=jnp.float32).astype(jnp.bfloat16)


def ready_kernel(halves, gain_ref, sw_ref, *rest):
    chunks, (packed_ref, flipped_ref, rows_ref) = rest[:halves], rest[halves:]
    channels = sw_ref.shape[0]
    rows = gather_rows(chunks, rows_ref, channels)
    packed_ref[...] = project_half(rows, gain_ref[...], sw_ref)
    for i in range(rows_ref.shape[0]):
        flipped_ref[i] = rows_ref[i].T


def ready(gain, weights, chunks, pixels):
    halves = len(chunks)
    per_device = chunks[0].shape[0]
    channels = weights.shape[0]
    kind = chunks[0].dtype
    half = pixels // 2
    return pl.pallas_call(
        functools.partial(ready_kernel, halves),
        out_shape=[
            pltpu.VMEM((per_device * half, weights.shape[1]), kind),
            pltpu.VMEM((per_device, channels, half), jnp.float32),
        ],
        in_specs=[pl.BlockSpec()] + [VMEM] * (1 + halves),
        out_specs=[VMEM] * 2,
        scratch_shapes=[pltpu.VMEM((per_device, half, channels), jnp.float32)],
        cost_estimate=pl.CostEstimate(
            flops=2 * per_device * half * channels * 3 * channels,
            bytes_accessed=2 << 20,
            transcendentals=0,
        ),
        compiler_params=pltpu.CompilerParams(vmem_limit_bytes=LIMIT),
        name="ready",
    )(gain.reshape(1, channels), weights, *chunks)


def spatial_kernel(halves, gain_ref, sw_ref, so_ref, packed_ref, flipped_ref, *rest):
    chunks, (out_ref, rows_ref, att_ref) = rest[:halves], rest[halves:]
    per_device, channels, pixels = out_ref.shape
    half = pixels // 2
    rows = gather_rows(chunks, rows_ref, channels)
    late = project_half(rows, gain_ref[...], sw_ref)
    blocks = [
        (i, tile, sides)
        for i in range(per_device)
        for tile in plan(channels)
        for sides in SIDES
    ]

    def part_of(frame, column, sides):
        return jnp.concatenate(
            [
                (late if side else packed_ref)[
                    frame * half : (frame + 1) * half, column : column + LANES
                ]
                for side in sides
            ],
            axis=0,
        )

    def score(i):
        frame, tile, sides = blocks[i]
        return lax.dot_general(
            stack_heads(part_of(frame, tile.query, sides), tile.held),
            part_of(frame, tile.key, (0, 1)),
            NT,
            preferred_element_type=jnp.float32,
        )

    def mix(i, weights, norm):
        frame, tile, sides = blocks[i]
        values = part_of(frame, tile.value, (0, 1))
        mixed = jnp.dot(weights, values, preferred_element_type=jnp.float32) * norm
        first = sides[0] * half
        att_ref[frame, first : first + len(sides) * half, tile.start : tile.start + tile.width] = (
            unstack_heads(mixed, tile.held)[:, : tile.width].astype(jnp.bfloat16)
        )

    pipelined(len(blocks), score, mix, SPATIAL_LEAD)
    upper = lax.axis_index("pix") // halves
    for i in range(per_device):
        update = lax.dot_general(so_ref[...], att_ref[i], NT, preferred_element_type=jnp.float32)
        here = pl.multiple_of(upper * half, half)
        there = pl.multiple_of((1 - upper) * half, half)
        out_ref[i, :, pl.ds(here, half)] = (flipped_ref[i] + update[:, :half]).astype(jnp.bfloat16)
        out_ref[i, :, pl.ds(there, half)] = (rows_ref[i].T + update[:, half:]).astype(jnp.bfloat16)


def spatial(gain, weights, out_matrix, packed, flipped, chunks, pixels):
    halves = len(chunks)
    per_device = chunks[0].shape[0]
    channels = out_matrix.shape[0]
    kind = chunks[0].dtype
    return pl.pallas_call(
        functools.partial(spatial_kernel, halves),
        out_shape=jax.ShapeDtypeStruct((per_device, channels, pixels), kind),
        in_specs=[pl.BlockSpec()] + [VMEM] * (4 + halves),
        out_specs=pl.BlockSpec(),
        scratch_shapes=[
            pltpu.VMEM((per_device, pixels // 2, channels), jnp.float32),
            pltpu.VMEM((per_device, pixels, channels), kind),
        ],
        cost_estimate=pl.CostEstimate(
            flops=2 * per_device * pixels * channels * (4 * channels + 2 * pixels),
            bytes_accessed=4 << 20,
            transcendentals=0,
        ),
        compiler_params=pltpu.CompilerParams(vmem_limit_bytes=LIMIT),
        name="spatial",
    )(gain.reshape(1, channels), weights, out_matrix, packed, flipped, *chunks)


def both_ways(pairs, count):
    target = [device ^ 1 for device in range(count)]
    for a, b in pairs:
        target[a], target[b] = b, a
    return list(enumerate(target))


def border_pairs(clips, pix_count, turn):
    pairs = [
        (a * pix_count + place, (a + 1) * pix_count + place)
        for a in range(turn, clips - 1, 2)
        for place in range(pix_count)
    ]
    return both_ways(pairs, clips * pix_count)


def body(
    latents,
    sampled,
    temporal_gain,
    temporal_qkv,
    temporal_out,
    spatial_gain,
    spatial_qkv,
    spatial_out,
):
    clips, pix_count = lax.axis_size("clip"), lax.axis_size("pix")
    pixels = latents.shape[1] * pix_count
    gathered = clips > DIRECT_CLIPS or clips & (clips - 1) != 0
    x, a, b, p = prep(latents, sampled, clips, not gathered)
    if gathered:
        soon, last = [], [lax.all_gather(p, "clip", axis=0, tiled=True)]
    else:
        soon, last = [], [p]
        for step in range(2, clips):
            pick = lax.ppermute(p, "clip", [(i, i ^ step) for i in range(clips)])
            (soon if step == 2 else last).append(pick)
    a = lax.ppermute(a, ("clip", "pix"), border_pairs(clips, pix_count, 0))
    b = lax.ppermute(b, ("clip", "pix"), border_pairs(clips, pix_count, 1))
    q, own, xg, tw, sw, to, so = local(
        x, temporal_gain, temporal_qkv, temporal_out, spatial_qkv, spatial_out
    )
    last = [b] + last
    early_held = sum(part.shape[0] for part in [a] + soon)
    late_held = sum(part.shape[0] for part in last)
    pairs = early(temporal_gain, tw, a, soon, latents.shape[1], up(early_held, 2))
    rest = ((q, own, xg), pairs, temporal_gain, tw, to)
    held = (clips, early_held, late_held, pix_count)
    halves = pix_count // 2
    *sends, late = temporal(*rest, last, *held, True)

    def swap(chunk, step):
        return lax.ppermute(chunk, "pix", [(i, i ^ step) for i in range(pix_count)])

    crossed = [swap(sends[k], halves + k) for k in range(halves)]
    kept = temporal(*rest, [late], *held, False)
    here = [kept[0]] + [swap(kept[k], k) for k in range(1, halves)]
    packed, flipped = ready(spatial_gain, sw, here, pixels)
    return spatial(spatial_gain, sw, so, packed, flipped, crossed, pixels).transpose(0, 2, 1)


def solution(mesh):
    placed = (P(("group", "clip"), "pix", None), P(("group", "clip")), P(), P(), P(), P(), P(), P())
    return jax.shard_map(
        body,
        mesh=mesh,
        in_specs=placed,
        out_specs=P(("group", "clip", "pix"), None, None),
        check_vma=False,
    )
```

```python
import functools
import math

import jax
import jax.numpy as jnp
from jax import lax
from jax.experimental import pallas as pl
from jax.experimental.pallas import tpu as pltpu
from jax.sharding import PartitionSpec as P

HEAD_DIM = 64
HALO = 4
SUB = 8
LANES = 128
NEG = -1e30
SHARPNESS = 1.0 / (math.sqrt(HEAD_DIM) * math.log(2.0))
DIRECT_CLIPS = 4
LIMIT = 24 << 20
LEAD = 8
SPATIAL_LEAD = 2
SIDES = ((0, 1),)
FAR = pl.BlockSpec(memory_space=pltpu.HBM)
VMEM = pl.BlockSpec(memory_space=pltpu.VMEM)
NT = (((1,), (1,)), ((), ()))


def far(array):
    return pltpu.with_memory_space_constraint(array, pltpu.HBM)


def up(count, step):
    return -(-count // step) * step


def tiles_of(channels):
    return [(start, min(LANES, channels - start)) for start in range(0, channels, LANES)]


class Tile:
    def __init__(self, query, key, value, start, width):
        self.query, self.key, self.value = query, key, value
        self.start, self.width = start, width
        self.held, self.head = width // HEAD_DIM, start // HEAD_DIM


def plan(channels):
    whole = channels // LANES * LANES
    tiles = [
        Tile(start, whole + start, 2 * whole + start, start, LANES) for start in range(0, whole, LANES)
    ]
    if channels > whole:
        tiles.append(Tile(3 * whole, 3 * whole + LANES, 3 * whole, whole, channels - whole))
    return tiles


def planned_width(channels):
    whole = channels // LANES * LANES
    return 3 * whole + (2 * LANES if channels > whole else 0)


def pack(rows):
    pixels, channels = rows.shape
    parts = [rows[:, start : start + width] for start, width in tiles_of(channels) if width == LANES]
    if channels % LANES:
        tail = rows[:, channels - channels % LANES :]
        parts.append(jnp.concatenate([tail[: pixels // 2], tail[pixels // 2 :]], axis=1))
    return jnp.concatenate(parts, axis=0)


def unpack(dense, pixels, channels):
    whole = channels // LANES
    parts = [dense[i * pixels : (i + 1) * pixels] for i in range(whole)]
    if channels % LANES:
        tail = dense[whole * pixels :]
        parts.append(jnp.concatenate([tail[:, : LANES // 2], tail[:, LANES // 2 :]], axis=0))
    return jnp.concatenate(parts, axis=1)


def layer_norm(values, scales):
    share = 1.0 / values.shape[-1]
    average = jnp.sum(values, axis=-1, keepdims=True) * share
    centred = values - average
    spread = jnp.sum(centred * centred, axis=-1, keepdims=True) * share
    return centred * lax.rsqrt(spread + 1e-05) * scales


def own_lanes(shape, slot):
    return (lax.broadcasted_iota(jnp.int32, shape, 1) // HEAD_DIM) == slot


def stack_heads(queries, held):
    if held == 1:
        return queries
    zero = jnp.zeros_like(queries)
    return jnp.concatenate(
        [jnp.where(own_lanes(queries.shape, slot), queries, zero) for slot in range(held)], axis=0
    )


def unstack_heads(mixed, held):
    rows = mixed.shape[0] // held
    result = mixed[:rows]
    for slot in range(1, held):
        part = mixed[slot * rows : (slot + 1) * rows]
        result = jnp.where(own_lanes(part.shape, slot), part, result)
    return result


def soften(scores):
    highest = jnp.max(scores, axis=-1, keepdims=True)
    expo = jnp.exp2((scores - highest) * SHARPNESS)
    return expo.astype(jnp.bfloat16), 1.0 / jnp.sum(expo, axis=-1, keepdims=True)


def pipelined(count, score, mix, lead=1):
    scores, weights = {}, {}
    for i in range(count + 2 * lead):
        if i < count:
            scores[i] = score(i)
        if 0 <= i - lead < count:
            weights[i - lead] = soften(scores.pop(i - lead))
        if 0 <= i - 2 * lead < count:
            mix(i - 2 * lead, *weights.pop(i - 2 * lead))


def neighbours(clips):
    me = lax.axis_index("clip")
    odd = lax.rem(me, 2)
    outer = jnp.where(odd == 1, me + 1, me - 1)
    inner = jnp.where(odd == 1, me - 1, me + 1)
    outer_there = (outer >= 0) & (outer < clips)
    inner_there = inner < clips
    return me, odd, inner_there, outer_there


def pick_kernel(x_hbm, s_ref, p_ref, frame_ref, sem):
    copy = pltpu.make_async_copy(x_hbm.at[s_ref[0]], frame_ref, sem)
    copy.start()
    copy.wait()
    p_ref[0] = pack(frame_ref[...])


def pick_frame(latents, sampled):
    _, pixels, channels = latents.shape
    kind = latents.dtype
    return pl.pallas_call(
        pick_kernel,
        out_shape=pltpu.VMEM((1, pixels * channels // LANES, LANES), kind),
        in_specs=[FAR, pl.BlockSpec(memory_space=pltpu.SMEM)],
        out_specs=VMEM,
        scratch_shapes=[pltpu.VMEM((pixels, channels), kind), pltpu.SemaphoreType.DMA],
        compiler_params=pltpu.CompilerParams(vmem_limit_bytes=LIMIT),
        name="pick",
    )(far(latents), sampled)


def prep_kernel(clips, x_ref, p_ref, a_ref, b_ref):
    _, odd, _, _ = neighbours(clips)
    span = x_ref.shape[0] - HALO
    for i in range(HALO):
        a_ref[i] = pack(x_ref[(1 - odd) * span + i])
        b_ref[i] = pack(x_ref[odd * span + i])
    if a_ref.shape[0] > HALO:
        a_ref[HALO] = p_ref[0]


def prep(latents, picked, clips, with_pick):
    dense = picked.shape[1:]
    kind = latents.dtype
    return pl.pallas_call(
        functools.partial(prep_kernel, clips),
        out_shape=[
            pltpu.VMEM((HALO + (1 if with_pick else 0),) + dense, kind),
            pltpu.VMEM((HALO,) + dense, kind),
        ],
        in_specs=[VMEM, VMEM],
        out_specs=[VMEM] * 2,
        compiler_params=pltpu.CompilerParams(vmem_limit_bytes=LIMIT),
        name="prep",
    )(latents, picked)


def local_kernel(
    x_ref, gain_ref, tq_hbm, to_hbm, sq_hbm, so_hbm,
    q_ref, kv_ref, xg_ref, tw_ref, sw_ref, to_ref, so_ref,
    tq_ref, sq_ref, sp_ref, normed_ref, sems,
):
    copies = [
        pltpu.make_async_copy(source, target, sems.at[i])
        for i, (source, target) in enumerate(
            ((tq_hbm, tq_ref), (sq_hbm, sq_ref), (to_hbm, to_ref), (so_hbm, sp_ref))
        )
    ]
    for copy in copies:
        copy.start()
    frames, pixels, channels = x_ref.shape
    groups = pixels // SUB
    gain = gain_ref[...]
    for f in range(frames):
        values = x_ref[f].astype(jnp.float32)
        normed = layer_norm(values, gain)
        for g in range(groups):
            xg_ref[g, f] = values[g * SUB : (g + 1) * SUB]
            normed_ref[g, f] = normed[g * SUB : (g + 1) * SUB]
    whole = channels // LANES * LANES

    def spread(source, target):
        parts = [source[:, i * channels : (i + 1) * channels] for i in range(3)]
        for i, part in enumerate(parts):
            target[:, i * whole : (i + 1) * whole] = part[:, :whole]
        if channels > whole:
            queries, keys, values = (part[:, whole:] for part in parts)
            tail = jnp.concatenate([values, queries], axis=1)
            target[:, 3 * whole : 3 * whole + LANES] = tail
            target[:, 3 * whole + LANES :] = jnp.concatenate([jnp.zeros_like(keys), keys], axis=1)

    copies[0].wait()
    spread(tq_ref, tw_ref)
    rows = normed_ref[...].reshape(groups * frames * SUB, channels).astype(jnp.bfloat16)
    packed = jnp.dot(rows, tw_ref[...], preferred_element_type=jnp.float32).astype(jnp.bfloat16)
    own = frames * SUB
    for g in range(groups):
        for tile in plan(channels):
            for half in range(2):
                at = g * own + half * (own // 2)
                stacked = stack_heads(
                    packed[at : at + own // 2, tile.query : tile.query + LANES], tile.held
                )
                first = tile.head * (own // 2)
                q_ref[g, half, first : first + stacked.shape[0], :] = stacked
    kv_ref[...] = packed[:, whole:]
    copies[1].wait()
    spread(sq_ref, sw_ref)
    copies[2].wait()
    copies[3].wait()
    so_ref[...] = sp_ref[...].T


def local(latents, gain, temporal_qkv, temporal_out, spatial_qkv, spatial_out):
    frames, pixels, channels = latents.shape
    groups = pixels // SUB
    count = frames * pixels
    kind = latents.dtype
    wide = (channels, planned_width(channels))
    square = (channels, channels)
    pair_width = wide[1] - channels // LANES * LANES
    return pl.pallas_call(
        local_kernel,
        out_shape=[pltpu.VMEM((groups, 2, channels // HEAD_DIM * frames * SUB // 2, LANES), kind)]
        + [pltpu.VMEM((count, pair_width), kind)]
        + [pltpu.VMEM((groups, frames, SUB, channels), jnp.float32)]
        + [pltpu.VMEM(wide, kind)] * 2
        + [pltpu.VMEM(square, kind)] * 2,
        in_specs=[VMEM, VMEM] + [FAR] * 4,
        out_specs=[VMEM] * 7,
        scratch_shapes=[
            pltpu.VMEM(temporal_qkv.shape, kind),
            pltpu.VMEM(spatial_qkv.shape, kind),
            pltpu.VMEM(square, kind),
            pltpu.VMEM((groups, frames, SUB, channels), jnp.float32),
            pltpu.SemaphoreType.DMA((4,)),
        ],
        cost_estimate=pl.CostEstimate(
            flops=2 * count * channels * 3 * channels, bytes_accessed=4 << 20, transcendentals=0
        ),
        compiler_params=pltpu.CompilerParams(vmem_limit_bytes=LIMIT),
        name="local",
    )(
        latents,
        gain.reshape(1, channels),
        *(far(w) for w in (temporal_qkv, temporal_out, spatial_qkv, spatial_out)),
    )


def remote_pairs(dense, gain, tw_ref, normed_ref, pixels):
    channels = gain.shape[1]
    groups, slots = normed_ref.shape[:2]
    for j, frame in enumerate(dense):
        normed = layer_norm(unpack(frame, pixels, channels).astype(jnp.float32), gain)
        for g in range(groups):
            normed_ref[g, j] = normed[g * SUB : (g + 1) * SUB]
    for j in range(len(dense), slots):
        for g in range(groups):
            normed_ref[g, j] = jnp.zeros((SUB, channels), jnp.float32)
    whole = channels // LANES * LANES
    rows = normed_ref[...].reshape(groups * slots * SUB, channels).astype(jnp.bfloat16)
    return jnp.dot(rows, tw_ref[:, whole:], preferred_element_type=jnp.float32).astype(jnp.bfloat16)


def early_kernel(gain_ref, tw_ref, a_ref, *rest):
    *pick_refs, kv_ref, normed_ref = rest
    dense = [a_ref[i] for i in range(a_ref.shape[0])]
    for ref in pick_refs:
        dense += [ref[i] for i in range(ref.shape[0])]
    pixels = normed_ref.shape[0] * SUB
    kv_ref[...] = remote_pairs(dense, gain_ref[...], tw_ref, normed_ref, pixels)


def early(gain, weights, a, picks, pixels, slots):
    channels = weights.shape[0]
    groups = pixels // SUB
    kind = weights.dtype
    return pl.pallas_call(
        early_kernel,
        out_shape=pltpu.VMEM((pixels * slots, weights.shape[1] - channels // LANES * LANES), kind),
        in_specs=[VMEM] + [VMEM] * (2 + len(picks)),
        out_specs=VMEM,
        scratch_shapes=[pltpu.VMEM((groups, slots, SUB, channels), jnp.float32)],
        cost_estimate=pl.CostEstimate(
            flops=2 * pixels * slots * channels * 2 * channels, bytes_accessed=2 << 20, transcendentals=0
        ),
        compiler_params=pltpu.CompilerParams(vmem_limit_bytes=LIMIT),
        name="early",
    )(gain.reshape(1, channels), weights, a, *picks)


def temporal_kernel(
    clips, early_held, late_held, pix_count, cross,
    q_ref, own_ref, xg_ref, kv_ref, gain_ref, tw_ref, to_ref, *rest,
):
    halves = pix_count // 2
    scratch = 4 if cross else 2
    last_refs, sends, rest = (
        rest[: len(rest) - halves - scratch],
        rest[len(rest) - halves - scratch : len(rest) - scratch],
        rest[len(rest) - scratch :],
    )
    groups, frames, _, channels = xg_ref.shape
    pixels = groups * SUB
    _, _, first_there, second_there = neighbours(clips)
    if cross:
        late_ref, normed_ref, att_ref, rows_ref = rest
        dense = [ref[i] for ref in last_refs for i in range(ref.shape[0])]
        late_ref[...] = remote_pairs(dense, gain_ref[...], tw_ref, normed_ref, pixels)
    else:
        (late_ref,) = last_refs
        att_ref, rows_ref = rest
    place = lax.axis_index("pix")
    upper = place // halves
    half = 1 - upper if cross else upper
    whole = channels // LANES * LANES

    part = frames // 2
    mine, own = part * SUB, frames * SUB
    soon, more = kv_ref.shape[0] // groups, late_ref.shape[0] // groups
    shape = (mine, own + soon + more)
    row = lax.broadcasted_iota(jnp.int32, shape, 0)
    column = lax.broadcasted_iota(jnp.int32, shape, 1)
    usable = lax.rem(row, SUB) == lax.rem(column, SUB)
    slot = column // SUB - frames
    usable &= (slot < 0) | (slot >= HALO) | first_there
    usable &= (slot < early_held) | (slot >= soon // SUB)
    usable &= (slot < soon // SUB) | (slot >= soon // SUB + HALO) | second_there
    usable &= slot < soon // SUB + late_held
    bias = jnp.where(usable, 0.0, NEG).astype(jnp.float32)

    blocks = [(g, tile) for g in range(groups) for tile in plan(channels)]

    def pairs_of(g, column):
        span = slice(column - whole, column - whole + LANES)
        return jnp.concatenate(
            [
                own_ref[g * own : (g + 1) * own, span],
                kv_ref[g * soon : (g + 1) * soon, span],
                late_ref[g * more : (g + 1) * more, span],
            ],
            axis=0,
        )

    def score(i):
        g, tile = blocks[i]
        queries = q_ref[g, half, tile.head * mine : (tile.head + tile.held) * mine, :]
        scores = lax.dot_general(
            queries, pairs_of(g, tile.key), NT, preferred_element_type=jnp.float32
        )
        return scores + jnp.concatenate([bias] * tile.held, axis=0)

    def mix(i, weights, norm):
        g, tile = blocks[i]
        mixed = jnp.dot(weights, pairs_of(g, tile.value), preferred_element_type=jnp.float32) * norm
        att_ref[g * mine : (g + 1) * mine, tile.start : tile.start + tile.width] = unstack_heads(
            mixed, tile.held
        )[:, : tile.width].astype(jnp.bfloat16)

    pipelined(len(blocks), score, mix, LEAD)
    update = jnp.dot(att_ref[...], to_ref[...], preferred_element_type=jnp.float32)
    for g in range(groups):
        for f in range(part):
            at = (g * part + f) * SUB
            rows_ref[f, g * SUB : (g + 1) * SUB] = xg_ref[g, half * part + f] + update[at : at + SUB]
    per_device = sends[0].shape[0]
    for k, ref in enumerate(sends):
        target = jnp.bitwise_xor(lax.rem(place, halves), k)
        for i in range(per_device):
            ref[i] = pack(rows_ref[target * per_device + i].astype(jnp.bfloat16))


def temporal(
    parts, pairs, gain, weights, out_matrix, last, clips, early_held, late_held, pix_count, cross
):
    q, own, xg = parts
    groups, frames, _, channels = xg.shape
    pixels = groups * SUB
    count = frames * pixels
    kind = q.dtype
    dense = (pixels * channels // LANES, LANES)
    out_shape = [pltpu.VMEM((frames // pix_count,) + dense, kind)] * (pix_count // 2)
    scratch = [
        pltpu.VMEM((count // 2, channels), kind),
        pltpu.VMEM((frames // 2, pixels, channels), jnp.float32),
    ]
    if cross:
        slots = up(late_held, 2)
        out_shape = out_shape + [pltpu.VMEM((pixels * slots, pairs.shape[1]), kind)]
        scratch = [pltpu.VMEM((groups, slots, SUB, channels), jnp.float32)] + scratch
    return pl.pallas_call(
        functools.partial(temporal_kernel, clips, early_held, late_held, pix_count, cross),
        out_shape=out_shape,
        in_specs=[VMEM] * 4 + [VMEM] + [VMEM] * (2 + len(last)),
        out_specs=[VMEM] * len(out_shape),
        scratch_shapes=scratch,
        cost_estimate=pl.CostEstimate(
            flops=2 * count * channels * 2 * channels, bytes_accessed=4 << 20, transcendentals=0
        ),
        compiler_params=pltpu.CompilerParams(vmem_limit_bytes=LIMIT),
        name="cross" if cross else "near",
    )(q, own, xg, pairs, gain.reshape(1, channels), weights, out_matrix, *last)


def gather_rows(chunks, rows_ref, channels):
    halves = len(chunks)
    per_device, half_pixels = rows_ref.shape[:2]
    each = half_pixels // halves
    place = lax.rem(lax.axis_index("pix"), halves)
    for k, ref in enumerate(chunks):
        at = pl.multiple_of(jnp.bitwise_xor(place, k) * each, each)
        for i in range(per_device):
            rows_ref[i, pl.ds(at, each), :] = unpack(ref[i], each, channels).astype(jnp.float32)
    return rows_ref[...].reshape(per_device * half_pixels, channels)


def project_half(rows, gain, sw_ref):
    normed = layer_norm(rows, gain).astype(jnp.bfloat16)
    return jnp.dot(normed, sw_ref[...], preferred_element_type=jnp.float32).astype(jnp.bfloat16)


def ready_kernel(halves, gain_ref, sw_ref, *rest):
    chunks, (packed_ref, flipped_ref, rows_ref) = rest[:halves], rest[halves:]
    channels = sw_ref.shape[0]
    rows = gather_rows(chunks, rows_ref, channels)
    packed_ref[...] = project_half(rows, gain_ref[...], sw_ref)
    for i in range(rows_ref.shape[0]):
        flipped_ref[i] = rows_ref[i].T


def ready(gain, weights, chunks, pixels):
    halves = len(chunks)
    per_device = chunks[0].shape[0]
    channels = weights.shape[0]
    kind = chunks[0].dtype
    half = pixels // 2
    return pl.pallas_call(
        functools.partial(ready_kernel, halves),
        out_shape=[
            pltpu.VMEM((per_device * half, weights.shape[1]), kind),
            pltpu.VMEM((per_device, channels, half), jnp.float32),
        ],
        in_specs=[VMEM] + [VMEM] * (1 + halves),
        out_specs=[VMEM] * 2,
        scratch_shapes=[pltpu.VMEM((per_device, half, channels), jnp.float32)],
        cost_estimate=pl.CostEstimate(
            flops=2 * per_device * half * channels * 3 * channels,
            bytes_accessed=2 << 20,
            transcendentals=0,
        ),
        compiler_params=pltpu.CompilerParams(vmem_limit_bytes=LIMIT),
        name="ready",
    )(gain.reshape(1, channels), weights, *chunks)


def spatial_kernel(halves, gain_ref, sw_ref, so_ref, packed_ref, flipped_ref, *rest):
    chunks, (out_ref, rows_ref, att_ref) = rest[:halves], rest[halves:]
    per_device, channels, pixels = out_ref.shape
    half = pixels // 2
    rows = gather_rows(chunks, rows_ref, channels)
    late = project_half(rows, gain_ref[...], sw_ref)
    blocks = [
        (i, tile, sides)
        for i in range(per_device)
        for tile in plan(channels)
        for sides in SIDES
    ]

    def part_of(frame, column, sides):
        return jnp.concatenate(
            [
                (late if side else packed_ref)[
                    frame * half : (frame + 1) * half, column : column + LANES
                ]
                for side in sides
            ],
            axis=0,
        )

    def score(i):
        frame, tile, sides = blocks[i]
        return lax.dot_general(
            stack_heads(part_of(frame, tile.query, sides), tile.held),
            part_of(frame, tile.key, (0, 1)),
            NT,
            preferred_element_type=jnp.float32,
        )

    def mix(i, weights, norm):
        frame, tile, sides = blocks[i]
        values = part_of(frame, tile.value, (0, 1))
        mixed = jnp.dot(weights, values, preferred_element_type=jnp.float32) * norm
        first = sides[0] * half
        att_ref[frame, first : first + len(sides) * half, tile.start : tile.start + tile.width] = (
            unstack_heads(mixed, tile.held)[:, : tile.width].astype(jnp.bfloat16)
        )

    pipelined(len(blocks), score, mix, SPATIAL_LEAD)
    upper = lax.axis_index("pix") // halves
    for i in range(per_device):
        update = lax.dot_general(so_ref[...], att_ref[i], NT, preferred_element_type=jnp.float32)
        here = pl.multiple_of(upper * half, half)
        there = pl.multiple_of((1 - upper) * half, half)
        out_ref[i, :, pl.ds(here, half)] = (flipped_ref[i] + update[:, :half]).astype(jnp.bfloat16)
        out_ref[i, :, pl.ds(there, half)] = (rows_ref[i].T + update[:, half:]).astype(jnp.bfloat16)


def spatial(gain, weights, out_matrix, packed, flipped, chunks, pixels):
    halves = len(chunks)
    per_device = chunks[0].shape[0]
    channels = out_matrix.shape[0]
    kind = chunks[0].dtype
    return pl.pallas_call(
        functools.partial(spatial_kernel, halves),
        out_shape=jax.ShapeDtypeStruct((per_device, channels, pixels), kind),
        in_specs=[VMEM] + [VMEM] * (4 + halves),
        out_specs=pl.BlockSpec(),
        scratch_shapes=[
            pltpu.VMEM((per_device, pixels // 2, channels), jnp.float32),
            pltpu.VMEM((per_device, pixels, channels), kind),
        ],
        cost_estimate=pl.CostEstimate(
            flops=2 * per_device * pixels * channels * (4 * channels + 2 * pixels),
            bytes_accessed=4 << 20,
            transcendentals=0,
        ),
        compiler_params=pltpu.CompilerParams(vmem_limit_bytes=LIMIT),
        name="spatial",
    )(gain.reshape(1, channels), weights, out_matrix, packed, flipped, *chunks)


def both_ways(pairs, count):
    target = [device ^ 1 for device in range(count)]
    for a, b in pairs:
        target[a], target[b] = b, a
    return list(enumerate(target))


def border_pairs(clips, pix_count, turn):
    pairs = [
        (a * pix_count + place, (a + 1) * pix_count + place)
        for a in range(turn, clips - 1, 2)
        for place in range(pix_count)
    ]
    return both_ways(pairs, clips * pix_count)


def body(
    latents,
    sampled,
    temporal_gain,
    temporal_qkv,
    temporal_out,
    spatial_gain,
    spatial_qkv,
    spatial_out,
):
    clips, pix_count = lax.axis_size("clip"), lax.axis_size("pix")
    pixels = latents.shape[1] * pix_count
    gathered = clips > DIRECT_CLIPS or clips & (clips - 1) != 0
    x = pltpu.with_memory_space_constraint(latents, pltpu.VMEM)
    p = pick_frame(latents, sampled)
    a, b = prep(x, p, clips, not gathered)
    if gathered:
        soon, last = [], [lax.all_gather(p, "clip", axis=0, tiled=True)]
    else:
        soon, last = [], [p]
        for step in range(2, clips):
            pick = lax.ppermute(p, "clip", [(i, i ^ step) for i in range(clips)])
            (soon if step == 2 else last).append(pick)
    a = lax.ppermute(a, ("clip", "pix"), border_pairs(clips, pix_count, 0))
    b = lax.ppermute(b, ("clip", "pix"), border_pairs(clips, pix_count, 1))
    q, own, xg, tw, sw, to, so = local(
        x, temporal_gain, temporal_qkv, temporal_out, spatial_qkv, spatial_out
    )
    last = [b] + last
    early_held = sum(part.shape[0] for part in [a] + soon)
    late_held = sum(part.shape[0] for part in last)
    pairs = early(temporal_gain, tw, a, soon, latents.shape[1], up(early_held, 2))
    rest = ((q, own, xg), pairs, temporal_gain, tw, to)
    held = (clips, early_held, late_held, pix_count)
    halves = pix_count // 2
    *sends, late = temporal(*rest, last, *held, True)

    def swap(chunk, step):
        return lax.ppermute(chunk, "pix", [(i, i ^ step) for i in range(pix_count)])

    crossed = [swap(sends[k], halves + k) for k in range(halves)]
    kept = temporal(*rest, [late], *held, False)
    here = [kept[0]] + [swap(kept[k], k) for k in range(1, halves)]
    packed, flipped = ready(spatial_gain, sw, here, pixels)
    return spatial(spatial_gain, sw, so, packed, flipped, crossed, pixels).transpose(0, 2, 1)


def solution(mesh):
    placed = (P(("group", "clip"), "pix", None), P(("group", "clip")), P(), P(), P(), P(), P(), P())
    return jax.shard_map(
        body,
        mesh=mesh,
        in_specs=placed,
        out_specs=P(("group", "clip", "pix"), None, None),
        check_vma=False,
    )
```

```python
import functools
import math

import jax
import jax.numpy as jnp
from jax import lax
from jax.experimental import pallas as pl
from jax.experimental.pallas import tpu as pltpu
from jax.sharding import PartitionSpec as P

HEAD_DIM = 64
HALO = 4
SUB = 8
LANES = 128
NEG = -1e30
DIRECT_CLIPS = 4
LIMIT = 24 << 20
LEAD = 8
SPATIAL_LEAD = 2
SIDES = ((0, 1),)
FAR = pl.BlockSpec(memory_space=pltpu.HBM)
VMEM = pl.BlockSpec(memory_space=pltpu.VMEM)
NT = (((1,), (1,)), ((), ()))


def far(array):
    return pltpu.with_memory_space_constraint(array, pltpu.HBM)


def up(count, step):
    return -(-count // step) * step


def tiles_of(channels):
    return [(start, min(LANES, channels - start)) for start in range(0, channels, LANES)]


class Tile:
    def __init__(self, query, key, value, start, width):
        self.query, self.key, self.value = query, key, value
        self.start, self.width = start, width
        self.held, self.head = width // HEAD_DIM, start // HEAD_DIM


def plan(channels):
    whole = channels // LANES * LANES
    tiles = [
        Tile(start, whole + start, 2 * whole + start, start, LANES) for start in range(0, whole, LANES)
    ]
    if channels > whole:
        tiles.append(Tile(3 * whole, 3 * whole + LANES, 3 * whole, whole, channels - whole))
    return tiles


def planned_width(channels):
    whole = channels // LANES * LANES
    return 3 * whole + (2 * LANES if channels > whole else 0)


def pack(rows):
    pixels, channels = rows.shape
    parts = [rows[:, start : start + width] for start, width in tiles_of(channels) if width == LANES]
    if channels % LANES:
        tail = rows[:, channels - channels % LANES :]
        parts.append(jnp.concatenate([tail[: pixels // 2], tail[pixels // 2 :]], axis=1))
    return jnp.concatenate(parts, axis=0)


def unpack(dense, pixels, channels):
    whole = channels // LANES
    parts = [dense[i * pixels : (i + 1) * pixels] for i in range(whole)]
    if channels % LANES:
        tail = dense[whole * pixels :]
        parts.append(jnp.concatenate([tail[:, : LANES // 2], tail[:, LANES // 2 :]], axis=0))
    return jnp.concatenate(parts, axis=1)


def layer_norm(values, scales):
    share = 1.0 / values.shape[-1]
    average = jnp.sum(values, axis=-1, keepdims=True) * share
    centred = values - average
    spread = jnp.sum(centred * centred, axis=-1, keepdims=True) * share
    return centred * lax.rsqrt(spread + 1e-05) * scales


def own_lanes(shape, slot):
    return (lax.broadcasted_iota(jnp.int32, shape, 1) // HEAD_DIM) == slot


def stack_heads(queries, held):
    if held == 1:
        return queries
    zero = jnp.zeros_like(queries)
    return jnp.concatenate(
        [jnp.where(own_lanes(queries.shape, slot), queries, zero) for slot in range(held)], axis=0
    )


def unstack_heads(mixed, held):
    rows = mixed.shape[0] // held
    result = mixed[:rows]
    for slot in range(1, held):
        part = mixed[slot * rows : (slot + 1) * rows]
        result = jnp.where(own_lanes(part.shape, slot), part, result)
    return result


def soften(scores):
    highest = jnp.max(scores, axis=-1, keepdims=True)
    expo = jnp.exp((scores - highest) * (1.0 / math.sqrt(HEAD_DIM)))
    return expo.astype(jnp.bfloat16), 1.0 / jnp.sum(expo, axis=-1, keepdims=True)


def pipelined(count, score, mix, lead=1):
    scores, weights = {}, {}
    for i in range(count + 2 * lead):
        if i < count:
            scores[i] = score(i)
        if 0 <= i - lead < count:
            weights[i - lead] = soften(scores.pop(i - lead))
        if 0 <= i - 2 * lead < count:
            mix(i - 2 * lead, *weights.pop(i - 2 * lead))


def neighbours(clips):
    me = lax.axis_index("clip")
    odd = lax.rem(me, 2)
    outer = jnp.where(odd == 1, me + 1, me - 1)
    inner = jnp.where(odd == 1, me - 1, me + 1)
    outer_there = (outer >= 0) & (outer < clips)
    inner_there = inner < clips
    return me, odd, inner_there, outer_there


def prep_kernel(clips, x_hbm, s_ref, x_ref, a_ref, b_ref, p_ref, x_sem):
    copy_x = pltpu.make_async_copy(x_hbm, x_ref, x_sem)
    copy_x.start()
    _, odd, _, _ = neighbours(clips)
    copy_x.wait()
    span = x_ref.shape[0] - HALO
    for i in range(HALO):
        a_ref[i] = pack(x_ref[(1 - odd) * span + i])
        b_ref[i] = pack(x_ref[odd * span + i])
    picked = pack(x_ref[s_ref[0]])
    p_ref[0] = picked
    if a_ref.shape[0] > HALO:
        a_ref[HALO] = picked


def prep(latents, sampled, clips, with_pick):
    _, pixels, channels = latents.shape
    dense = (pixels * channels // LANES, LANES)
    sent = HALO + (1 if with_pick else 0)
    kind = latents.dtype
    return pl.pallas_call(
        functools.partial(prep_kernel, clips),
        out_shape=[
            pltpu.VMEM(latents.shape, kind),
            pltpu.VMEM((sent,) + dense, kind),
            pltpu.VMEM((HALO,) + dense, kind),
            pltpu.VMEM((1,) + dense, kind),
        ],
        in_specs=[FAR, pl.BlockSpec(memory_space=pltpu.SMEM)],
        out_specs=[VMEM] * 4,
        scratch_shapes=[pltpu.SemaphoreType.DMA],
        compiler_params=pltpu.CompilerParams(vmem_limit_bytes=LIMIT),
        name="prep",
    )(far(latents), sampled)


def local_kernel(
    x_ref, gain_ref, tq_hbm, to_hbm, sq_hbm, so_hbm,
    q_ref, kv_ref, xg_ref, tw_ref, sw_ref, to_ref, so_ref,
    tq_ref, sq_ref, sp_ref, normed_ref, sems,
):
    copies = [
        pltpu.make_async_copy(source, target, sems.at[i])
        for i, (source, target) in enumerate(
            ((tq_hbm, tq_ref), (sq_hbm, sq_ref), (to_hbm, to_ref), (so_hbm, sp_ref))
        )
    ]
    for copy in copies:
        copy.start()
    frames, pixels, channels = x_ref.shape
    groups = pixels // SUB
    gain = gain_ref[...]
    for f in range(frames):
        values = x_ref[f].astype(jnp.float32)
        normed = layer_norm(values, gain)
        for g in range(groups):
            xg_ref[g, f] = values[g * SUB : (g + 1) * SUB]
            normed_ref[g, f] = normed[g * SUB : (g + 1) * SUB]
    whole = channels // LANES * LANES

    def spread(source, target):
        parts = [source[:, i * channels : (i + 1) * channels] for i in range(3)]
        for i, part in enumerate(parts):
            target[:, i * whole : (i + 1) * whole] = part[:, :whole]
        if channels > whole:
            queries, keys, values = (part[:, whole:] for part in parts)
            tail = jnp.concatenate([values, queries], axis=1)
            target[:, 3 * whole : 3 * whole + LANES] = tail
            target[:, 3 * whole + LANES :] = jnp.concatenate([jnp.zeros_like(keys), keys], axis=1)

    copies[0].wait()
    spread(tq_ref, tw_ref)
    rows = normed_ref[...].reshape(groups * frames * SUB, channels).astype(jnp.bfloat16)
    packed = jnp.dot(rows, tw_ref[...], preferred_element_type=jnp.float32).astype(jnp.bfloat16)
    own = frames * SUB
    for g in range(groups):
        for tile in plan(channels):
            for half in range(2):
                at = g * own + half * (own // 2)
                stacked = stack_heads(
                    packed[at : at + own // 2, tile.query : tile.query + LANES], tile.held
                )
                first = tile.head * (own // 2)
                q_ref[g, half, first : first + stacked.shape[0], :] = stacked
    kv_ref[...] = packed[:, whole:]
    copies[1].wait()
    spread(sq_ref, sw_ref)
    copies[2].wait()
    copies[3].wait()
    so_ref[...] = sp_ref[...].T


def local(latents, gain, temporal_qkv, temporal_out, spatial_qkv, spatial_out):
    frames, pixels, channels = latents.shape
    groups = pixels // SUB
    count = frames * pixels
    kind = latents.dtype
    wide = (channels, planned_width(channels))
    square = (channels, channels)
    pair_width = wide[1] - channels // LANES * LANES
    return pl.pallas_call(
        local_kernel,
        out_shape=[pltpu.VMEM((groups, 2, channels // HEAD_DIM * frames * SUB // 2, LANES), kind)]
        + [pltpu.VMEM((count, pair_width), kind)]
        + [pltpu.VMEM((groups, frames, SUB, channels), jnp.float32)]
        + [pltpu.VMEM(wide, kind)] * 2
        + [pltpu.VMEM(square, kind)] * 2,
        in_specs=[VMEM, pl.BlockSpec()] + [FAR] * 4,
        out_specs=[VMEM] * 7,
        scratch_shapes=[
            pltpu.VMEM(temporal_qkv.shape, kind),
            pltpu.VMEM(spatial_qkv.shape, kind),
            pltpu.VMEM(square, kind),
            pltpu.VMEM((groups, frames, SUB, channels), jnp.float32),
            pltpu.SemaphoreType.DMA((4,)),
        ],
        cost_estimate=pl.CostEstimate(
            flops=2 * count * channels * 3 * channels, bytes_accessed=4 << 20, transcendentals=0
        ),
        compiler_params=pltpu.CompilerParams(vmem_limit_bytes=LIMIT),
        name="local",
    )(
        latents,
        gain.reshape(1, channels),
        *(far(w) for w in (temporal_qkv, temporal_out, spatial_qkv, spatial_out)),
    )


def remote_pairs(dense, gain, tw_ref, normed_ref, pixels):
    channels = gain.shape[1]
    groups, slots = normed_ref.shape[:2]
    for j, frame in enumerate(dense):
        normed = layer_norm(unpack(frame, pixels, channels).astype(jnp.float32), gain)
        for g in range(groups):
            normed_ref[g, j] = normed[g * SUB : (g + 1) * SUB]
    for j in range(len(dense), slots):
        for g in range(groups):
            normed_ref[g, j] = jnp.zeros((SUB, channels), jnp.float32)
    whole = channels // LANES * LANES
    rows = normed_ref[...].reshape(groups * slots * SUB, channels).astype(jnp.bfloat16)
    return jnp.dot(rows, tw_ref[:, whole:], preferred_element_type=jnp.float32).astype(jnp.bfloat16)


def early_kernel(gain_ref, tw_ref, *rest):
    *refs, kv_ref, normed_ref = rest
    dense = [ref[i] for ref in refs for i in range(min(HALO, ref.shape[0]))]
    pixels = normed_ref.shape[0] * SUB
    kv_ref[...] = remote_pairs(dense, gain_ref[...], tw_ref, normed_ref, pixels)


def early(gain, weights, frames, pixels, slots):
    channels = weights.shape[0]
    groups = pixels // SUB
    kind = weights.dtype
    return pl.pallas_call(
        early_kernel,
        out_shape=pltpu.VMEM((pixels * slots, weights.shape[1] - channels // LANES * LANES), kind),
        in_specs=[pl.BlockSpec()] + [VMEM] * (1 + len(frames)),
        out_specs=VMEM,
        scratch_shapes=[pltpu.VMEM((groups, slots, SUB, channels), jnp.float32)],
        cost_estimate=pl.CostEstimate(
            flops=2 * pixels * slots * channels * 2 * channels, bytes_accessed=2 << 20, transcendentals=0
        ),
        compiler_params=pltpu.CompilerParams(vmem_limit_bytes=LIMIT),
        name="early",
    )(gain.reshape(1, channels), weights, *frames)


def temporal_kernel(
    clips, ahead, early_held, late_held, pix_count, cross,
    q_ref, own_ref, xg_ref, kv_ref, gain_ref, tw_ref, to_ref, *rest,
):
    halves = pix_count // 2
    scratch = 4 if cross else 2
    before_refs, rest = rest[:ahead], rest[ahead:]
    last_refs, sends, rest = (
        rest[: len(rest) - halves - scratch],
        rest[len(rest) - halves - scratch : len(rest) - scratch],
        rest[len(rest) - scratch :],
    )
    groups, frames, _, channels = xg_ref.shape
    pixels = groups * SUB
    _, _, first_there, second_there = neighbours(clips)
    if cross:
        late_ref, normed_ref, att_ref, rows_ref = rest
        dense = [ref[i] for ref in last_refs for i in range(HALO if ref.shape[0] == HALO + 1 else 0, ref.shape[0])]
        late_ref[...] = remote_pairs(dense, gain_ref[...], tw_ref, normed_ref, pixels)
    else:
        (late_ref,) = last_refs
        att_ref, rows_ref = rest
    place = lax.axis_index("pix")
    upper = place // halves
    half = 1 - upper if cross else upper
    whole = channels // LANES * LANES

    part = frames // 2
    mine, own = part * SUB, frames * SUB
    soon, more = kv_ref.shape[0] // groups, late_ref.shape[0] // groups
    sooner = sum(ref.shape[0] for ref in before_refs) // groups
    shape = (mine, own + sooner + soon + more)
    row = lax.broadcasted_iota(jnp.int32, shape, 0)
    column = lax.broadcasted_iota(jnp.int32, shape, 1)
    usable = lax.rem(row, SUB) == lax.rem(column, SUB)
    slot = (column - sooner) // SUB - frames
    usable &= (slot < 0) | (slot >= HALO) | first_there
    usable &= (slot < early_held) | (slot >= soon // SUB)
    usable &= (slot < soon // SUB) | (slot >= soon // SUB + HALO) | second_there
    usable &= slot < soon // SUB + late_held
    bias = jnp.where(usable, 0.0, NEG).astype(jnp.float32)

    blocks = [(g, tile) for g in range(groups) for tile in plan(channels)]

    def pairs_of(g, column):
        span = slice(column - whole, column - whole + LANES)
        return jnp.concatenate(
            [
                own_ref[g * own : (g + 1) * own, span],
                *(ref[g * sooner : (g + 1) * sooner, span] for ref in before_refs),
                kv_ref[g * soon : (g + 1) * soon, span],
                late_ref[g * more : (g + 1) * more, span],
            ],
            axis=0,
        )

    def score(i):
        g, tile = blocks[i]
        queries = q_ref[g, half, tile.head * mine : (tile.head + tile.held) * mine, :]
        scores = lax.dot_general(
            queries, pairs_of(g, tile.key), NT, preferred_element_type=jnp.float32
        )
        return scores + jnp.concatenate([bias] * tile.held, axis=0)

    def mix(i, weights, norm):
        g, tile = blocks[i]
        mixed = jnp.dot(weights, pairs_of(g, tile.value), preferred_element_type=jnp.float32) * norm
        att_ref[g * mine : (g + 1) * mine, tile.start : tile.start + tile.width] = unstack_heads(
            mixed, tile.held
        )[:, : tile.width].astype(jnp.bfloat16)

    pipelined(len(blocks), score, mix, LEAD)
    update = jnp.dot(att_ref[...], to_ref[...], preferred_element_type=jnp.float32)
    for g in range(groups):
        for f in range(part):
            at = (g * part + f) * SUB
            rows_ref[f, g * SUB : (g + 1) * SUB] = xg_ref[g, half * part + f] + update[at : at + SUB]
    per_device = sends[0].shape[0]
    for k, ref in enumerate(sends):
        target = jnp.bitwise_xor(lax.rem(place, halves), k)
        for i in range(per_device):
            ref[i] = pack(rows_ref[target * per_device + i].astype(jnp.bfloat16))


def temporal(
    parts, pairs, gain, weights, out_matrix, before, last, clips, early_held, late_held, pix_count, cross
):
    q, own, xg = parts
    groups, frames, _, channels = xg.shape
    pixels = groups * SUB
    count = frames * pixels
    kind = q.dtype
    dense = (pixels * channels // LANES, LANES)
    out_shape = [pltpu.VMEM((frames // pix_count,) + dense, kind)] * (pix_count // 2)
    scratch = [
        pltpu.VMEM((count // 2, channels), kind),
        pltpu.VMEM((frames // 2, pixels, channels), jnp.float32),
    ]
    if cross:
        slots = up(late_held, 2)
        out_shape = out_shape + [pltpu.VMEM((pixels * slots, pairs.shape[1]), kind)]
        scratch = [pltpu.VMEM((groups, slots, SUB, channels), jnp.float32)] + scratch
    return pl.pallas_call(
        functools.partial(temporal_kernel, clips, len(before), early_held, late_held, pix_count, cross),
        out_shape=out_shape,
        in_specs=[VMEM] * 4 + [pl.BlockSpec()] + [VMEM] * (2 + len(before) + len(last)),
        out_specs=[VMEM] * len(out_shape),
        scratch_shapes=scratch,
        cost_estimate=pl.CostEstimate(
            flops=2 * count * channels * 2 * channels, bytes_accessed=4 << 20, transcendentals=0
        ),
        compiler_params=pltpu.CompilerParams(vmem_limit_bytes=LIMIT),
        name="cross" if cross else "near",
    )(q, own, xg, pairs, gain.reshape(1, channels), weights, out_matrix, *before, *last)


def gather_rows(chunks, rows_ref, channels):
    halves = len(chunks)
    per_device, half_pixels = rows_ref.shape[:2]
    each = half_pixels // halves
    place = lax.rem(lax.axis_index("pix"), halves)
    for k, ref in enumerate(chunks):
        at = pl.multiple_of(jnp.bitwise_xor(place, k) * each, each)
        for i in range(per_device):
            rows_ref[i, pl.ds(at, each), :] = unpack(ref[i], each, channels).astype(jnp.float32)
    return rows_ref[...].reshape(per_device * half_pixels, channels)


def project_half(rows, gain, sw_ref):
    normed = layer_norm(rows, gain).astype(jnp.bfloat16)
    return jnp.dot(normed, sw_ref[...], preferred_element_type=jnp.float32).astype(jnp.bfloat16)


def ready_kernel(halves, gain_ref, sw_ref, *rest):
    chunks, (packed_ref, flipped_ref, rows_ref) = rest[:halves], rest[halves:]
    channels = sw_ref.shape[0]
    rows = gather_rows(chunks, rows_ref, channels)
    packed_ref[...] = project_half(rows, gain_ref[...], sw_ref)
    for i in range(rows_ref.shape[0]):
        flipped_ref[i] = rows_ref[i].T


def ready(gain, weights, chunks, pixels):
    halves = len(chunks)
    per_device = chunks[0].shape[0]
    channels = weights.shape[0]
    kind = chunks[0].dtype
    half = pixels // 2
    return pl.pallas_call(
        functools.partial(ready_kernel, halves),
        out_shape=[
            pltpu.VMEM((per_device * half, weights.shape[1]), kind),
            pltpu.VMEM((per_device, channels, half), jnp.float32),
        ],
        in_specs=[pl.BlockSpec()] + [VMEM] * (1 + halves),
        out_specs=[VMEM] * 2,
        scratch_shapes=[pltpu.VMEM((per_device, half, channels), jnp.float32)],
        cost_estimate=pl.CostEstimate(
            flops=2 * per_device * half * channels * 3 * channels,
            bytes_accessed=2 << 20,
            transcendentals=0,
        ),
        compiler_params=pltpu.CompilerParams(vmem_limit_bytes=LIMIT),
        name="ready",
    )(gain.reshape(1, channels), weights, *chunks)


def spatial_kernel(halves, gain_ref, sw_ref, so_ref, packed_ref, flipped_ref, *rest):
    chunks, (out_ref, rows_ref, att_ref) = rest[:halves], rest[halves:]
    per_device, channels, pixels = out_ref.shape
    half = pixels // 2
    rows = gather_rows(chunks, rows_ref, channels)
    late = project_half(rows, gain_ref[...], sw_ref)
    blocks = [
        (i, tile, sides)
        for i in range(per_device)
        for tile in plan(channels)
        for sides in SIDES
    ]

    def part_of(frame, column, sides):
        return jnp.concatenate(
            [
                (late if side else packed_ref)[
                    frame * half : (frame + 1) * half, column : column + LANES
                ]
                for side in sides
            ],
            axis=0,
        )

    def score(i):
        frame, tile, sides = blocks[i]
        return lax.dot_general(
            stack_heads(part_of(frame, tile.query, sides), tile.held),
            part_of(frame, tile.key, (0, 1)),
            NT,
            preferred_element_type=jnp.float32,
        )

    def mix(i, weights, norm):
        frame, tile, sides = blocks[i]
        values = part_of(frame, tile.value, (0, 1))
        mixed = jnp.dot(weights, values, preferred_element_type=jnp.float32) * norm
        first = sides[0] * half
        att_ref[frame, first : first + len(sides) * half, tile.start : tile.start + tile.width] = (
            unstack_heads(mixed, tile.held)[:, : tile.width].astype(jnp.bfloat16)
        )

    pipelined(len(blocks), score, mix, SPATIAL_LEAD)
    upper = lax.axis_index("pix") // halves
    for i in range(per_device):
        update = lax.dot_general(so_ref[...], att_ref[i], NT, preferred_element_type=jnp.float32)
        here = pl.multiple_of(upper * half, half)
        there = pl.multiple_of((1 - upper) * half, half)
        out_ref[i, :, pl.ds(here, half)] = (flipped_ref[i] + update[:, :half]).astype(jnp.bfloat16)
        out_ref[i, :, pl.ds(there, half)] = (rows_ref[i].T + update[:, half:]).astype(jnp.bfloat16)


def spatial(gain, weights, out_matrix, packed, flipped, chunks, pixels):
    halves = len(chunks)
    per_device = chunks[0].shape[0]
    channels = out_matrix.shape[0]
    kind = chunks[0].dtype
    return pl.pallas_call(
        functools.partial(spatial_kernel, halves),
        out_shape=jax.ShapeDtypeStruct((per_device, channels, pixels), kind),
        in_specs=[pl.BlockSpec()] + [VMEM] * (4 + halves),
        out_specs=pl.BlockSpec(),
        scratch_shapes=[
            pltpu.VMEM((per_device, pixels // 2, channels), jnp.float32),
            pltpu.VMEM((per_device, pixels, channels), kind),
        ],
        cost_estimate=pl.CostEstimate(
            flops=2 * per_device * pixels * channels * (4 * channels + 2 * pixels),
            bytes_accessed=4 << 20,
            transcendentals=0,
        ),
        compiler_params=pltpu.CompilerParams(vmem_limit_bytes=LIMIT),
        name="spatial",
    )(gain.reshape(1, channels), weights, out_matrix, packed, flipped, *chunks)


def both_ways(pairs, count):
    target = [device ^ 1 for device in range(count)]
    for a, b in pairs:
        target[a], target[b] = b, a
    return list(enumerate(target))


def border_pairs(clips, pix_count, turn):
    pairs = [
        (a * pix_count + place, (a + 1) * pix_count + place)
        for a in range(turn, clips - 1, 2)
        for place in range(pix_count)
    ]
    return both_ways(pairs, clips * pix_count)


def body(
    latents,
    sampled,
    temporal_gain,
    temporal_qkv,
    temporal_out,
    spatial_gain,
    spatial_qkv,
    spatial_out,
):
    clips, pix_count = lax.axis_size("clip"), lax.axis_size("pix")
    pixels = latents.shape[1] * pix_count
    gathered = clips > DIRECT_CLIPS or clips & (clips - 1) != 0
    x, a, b, p = prep(latents, sampled, clips, not gathered)
    if gathered:
        soon, last = [], [lax.all_gather(p, "clip", axis=0, tiled=True)]
    else:
        soon, last = [], [p]
        for step in range(2, clips):
            pick = lax.ppermute(p, "clip", [(i, i ^ step) for i in range(clips)])
            (soon if step == 2 else last).append(pick)
    a = lax.ppermute(a, ("clip", "pix"), border_pairs(clips, pix_count, 0))
    b = lax.ppermute(b, ("clip", "pix"), border_pairs(clips, pix_count, 1))
    q, own, xg, tw, sw, to, so = local(
        x, temporal_gain, temporal_qkv, temporal_out, spatial_qkv, spatial_out
    )
    each, before = latents.shape[1], []
    if not gathered:
        before = [early(temporal_gain, tw, soon + last[:1], each, up(len(soon) + 1, 2))]
        last = last[1:] + [a]
    last = [b] + last
    late_held = sum(1 if part is a else part.shape[0] for part in last)
    pairs = early(temporal_gain, tw, [a], each, up(HALO, 2))
    rest = ((q, own, xg), pairs, temporal_gain, tw, to, before)
    held = (clips, HALO, late_held, pix_count)
    halves = pix_count // 2
    *sends, late = temporal(*rest, last, *held, True)

    def swap(chunk, step):
        return lax.ppermute(chunk, "pix", [(i, i ^ step) for i in range(pix_count)])

    crossed = [swap(sends[k], halves + k) for k in range(halves)]
    kept = temporal(*rest, [late], *held, False)
    here = [kept[0]] + [swap(kept[k], k) for k in range(1, halves)]
    packed, flipped = ready(spatial_gain, sw, here, pixels)
    return spatial(spatial_gain, sw, so, packed, flipped, crossed, pixels).transpose(0, 2, 1)


def solution(mesh):
    placed = (P(("group", "clip"), "pix", None), P(("group", "clip")), P(), P(), P(), P(), P(), P())
    return jax.shard_map(
        body,
        mesh=mesh,
        in_specs=placed,
        out_specs=P(("group", "clip", "pix"), None, None),
        check_vma=False,
    )
```

```python
import functools
import math

import jax
import jax.numpy as jnp
from jax import lax
from jax.experimental import pallas as pl
from jax.experimental.pallas import tpu as pltpu
from jax.sharding import PartitionSpec as P

HEAD_DIM = 64
HALO = 4
SUB = 8
LANES = 128
NEG = -1e30
SHARPNESS = 1.0 / (math.sqrt(HEAD_DIM) * math.log(2.0))
DIRECT_CLIPS = 4
LIMIT = 24 << 20
LEAD = 12
SPATIAL_LEAD = 2
SIDES = ((0, 1),)
FAR = pl.BlockSpec(memory_space=pltpu.HBM)
VMEM = pl.BlockSpec(memory_space=pltpu.VMEM)
NT = (((1,), (1,)), ((), ()))


def far(array):
    return pltpu.with_memory_space_constraint(array, pltpu.HBM)


def up(count, step):
    return -(-count // step) * step


def tiles_of(channels):
    return [(start, min(LANES, channels - start)) for start in range(0, channels, LANES)]


class Tile:
    def __init__(self, query, key, value, start, width):
        self.query, self.key, self.value = query, key, value
        self.start, self.width = start, width
        self.held, self.head = width // HEAD_DIM, start // HEAD_DIM


def plan(channels):
    whole = channels // LANES * LANES
    tiles = [
        Tile(start, whole + start, 2 * whole + start, start, LANES) for start in range(0, whole, LANES)
    ]
    if channels > whole:
        tiles.append(Tile(3 * whole, 3 * whole + LANES, 3 * whole, whole, channels - whole))
    return tiles


def planned_width(channels):
    whole = channels // LANES * LANES
    return 3 * whole + (2 * LANES if channels > whole else 0)


def pack(rows):
    pixels, channels = rows.shape
    parts = [rows[:, start : start + width] for start, width in tiles_of(channels) if width == LANES]
    if channels % LANES:
        tail = rows[:, channels - channels % LANES :]
        parts.append(jnp.concatenate([tail[: pixels // 2], tail[pixels // 2 :]], axis=1))
    return jnp.concatenate(parts, axis=0)


def unpack(dense, pixels, channels):
    whole = channels // LANES
    parts = [dense[i * pixels : (i + 1) * pixels] for i in range(whole)]
    if channels % LANES:
        tail = dense[whole * pixels :]
        parts.append(jnp.concatenate([tail[:, : LANES // 2], tail[:, LANES // 2 :]], axis=0))
    return jnp.concatenate(parts, axis=1)


def layer_norm(values, scales):
    share = 1.0 / values.shape[-1]
    average = jnp.sum(values, axis=-1, keepdims=True) * share
    centred = values - average
    spread = jnp.sum(centred * centred, axis=-1, keepdims=True) * share
    return centred * lax.rsqrt(spread + 1e-05) * scales


def own_lanes(shape, slot):
    return (lax.broadcasted_iota(jnp.int32, shape, 1) // HEAD_DIM) == slot


def stack_heads(queries, held):
    if held == 1:
        return queries
    zero = jnp.zeros_like(queries)
    return jnp.concatenate(
        [jnp.where(own_lanes(queries.shape, slot), queries, zero) for slot in range(held)], axis=0
    )


def unstack_heads(mixed, held):
    rows = mixed.shape[0] // held
    result = mixed[:rows]
    for slot in range(1, held):
        part = mixed[slot * rows : (slot + 1) * rows]
        result = jnp.where(own_lanes(part.shape, slot), part, result)
    return result


def soften(scores):
    highest = jnp.max(scores, axis=-1, keepdims=True)
    expo = jnp.exp2((scores - highest) * SHARPNESS)
    return expo.astype(jnp.bfloat16), 1.0 / jnp.sum(expo, axis=-1, keepdims=True)


def pipelined(count, score, mix, lead=1):
    scores, weights = {}, {}
    for i in range(count + 2 * lead):
        if i < count:
            scores[i] = score(i)
        if 0 <= i - lead < count:
            weights[i - lead] = soften(scores.pop(i - lead))
        if 0 <= i - 2 * lead < count:
            mix(i - 2 * lead, *weights.pop(i - 2 * lead))


def neighbours(clips):
    me = lax.axis_index("clip")
    odd = lax.rem(me, 2)
    outer = jnp.where(odd == 1, me + 1, me - 1)
    inner = jnp.where(odd == 1, me - 1, me + 1)
    outer_there = (outer >= 0) & (outer < clips)
    inner_there = inner < clips
    return me, odd, inner_there, outer_there


def pick_kernel(x_hbm, s_ref, p_ref, frame_ref, sem):
    copy = pltpu.make_async_copy(x_hbm.at[s_ref[0]], frame_ref, sem)
    copy.start()
    copy.wait()
    p_ref[0] = pack(frame_ref[...])


def pick_frame(latents, sampled):
    _, pixels, channels = latents.shape
    kind = latents.dtype
    return pl.pallas_call(
        pick_kernel,
        out_shape=pltpu.VMEM((1, pixels * channels // LANES, LANES), kind),
        in_specs=[FAR, pl.BlockSpec(memory_space=pltpu.SMEM)],
        out_specs=VMEM,
        scratch_shapes=[pltpu.VMEM((pixels, channels), kind), pltpu.SemaphoreType.DMA],
        compiler_params=pltpu.CompilerParams(vmem_limit_bytes=LIMIT),
        name="pick",
    )(far(latents), sampled)


def prep_kernel(clips, x_ref, p_ref, a_ref, b_ref):
    _, odd, _, _ = neighbours(clips)
    span = x_ref.shape[0] - HALO
    for i in range(HALO):
        a_ref[i] = pack(x_ref[(1 - odd) * span + i])
        b_ref[i] = pack(x_ref[odd * span + i])
    if a_ref.shape[0] > HALO:
        a_ref[HALO] = p_ref[0]


def prep(latents, picked, clips, with_pick):
    dense = picked.shape[1:]
    kind = latents.dtype
    return pl.pallas_call(
        functools.partial(prep_kernel, clips),
        out_shape=[
            pltpu.VMEM((HALO + (1 if with_pick else 0),) + dense, kind),
            pltpu.VMEM((HALO,) + dense, kind),
        ],
        in_specs=[VMEM, VMEM],
        out_specs=[VMEM] * 2,
        compiler_params=pltpu.CompilerParams(vmem_limit_bytes=LIMIT),
        name="prep",
    )(latents, picked)


def local_kernel(
    x_ref, gain_ref, tq_hbm, to_hbm, sq_hbm, so_hbm,
    q_ref, kv_ref, xg_ref, tw_ref, sw_ref, to_ref, so_ref,
    tq_ref, sq_ref, sp_ref, normed_ref, sems,
):
    copies = [
        pltpu.make_async_copy(source, target, sems.at[i])
        for i, (source, target) in enumerate(
            ((tq_hbm, tq_ref), (sq_hbm, sq_ref), (to_hbm, to_ref), (so_hbm, sp_ref))
        )
    ]
    for copy in copies:
        copy.start()
    frames, pixels, channels = x_ref.shape
    groups = pixels // SUB
    gain = gain_ref[...]
    for f in range(frames):
        values = x_ref[f].astype(jnp.float32)
        normed = layer_norm(values, gain)
        for g in range(groups):
            xg_ref[g, f] = values[g * SUB : (g + 1) * SUB]
            normed_ref[g, f] = normed[g * SUB : (g + 1) * SUB]
    whole = channels // LANES * LANES

    def spread(source, target):
        parts = [source[:, i * channels : (i + 1) * channels] for i in range(3)]
        for i, part in enumerate(parts):
            target[:, i * whole : (i + 1) * whole] = part[:, :whole]
        if channels > whole:
            queries, keys, values = (part[:, whole:] for part in parts)
            tail = jnp.concatenate([values, queries], axis=1)
            target[:, 3 * whole : 3 * whole + LANES] = tail
            target[:, 3 * whole + LANES :] = jnp.concatenate([jnp.zeros_like(keys), keys], axis=1)

    copies[0].wait()
    spread(tq_ref, tw_ref)
    rows = normed_ref[...].reshape(groups * frames * SUB, channels).astype(jnp.bfloat16)
    packed = jnp.dot(rows, tw_ref[...], preferred_element_type=jnp.float32).astype(jnp.bfloat16)
    own = frames * SUB
    for g in range(groups):
        for tile in plan(channels):
            for half in range(2):
                at = g * own + half * (own // 2)
                stacked = stack_heads(
                    packed[at : at + own // 2, tile.query : tile.query + LANES], tile.held
                )
                first = tile.head * (own // 2)
                q_ref[g, half, first : first + stacked.shape[0], :] = stacked
    kv_ref[...] = packed[:, whole:]
    copies[1].wait()
    spread(sq_ref, sw_ref)
    copies[2].wait()
    copies[3].wait()
    so_ref[...] = sp_ref[...].T


def local(latents, gain, temporal_qkv, temporal_out, spatial_qkv, spatial_out):
    frames, pixels, channels = latents.shape
    groups = pixels // SUB
    count = frames * pixels
    kind = latents.dtype
    wide = (channels, planned_width(channels))
    square = (channels, channels)
    pair_width = wide[1] - channels // LANES * LANES
    return pl.pallas_call(
        local_kernel,
        out_shape=[pltpu.VMEM((groups, 2, channels // HEAD_DIM * frames * SUB // 2, LANES), kind)]
        + [pltpu.VMEM((count, pair_width), kind)]
        + [pltpu.VMEM((groups, frames, SUB, channels), jnp.float32)]
        + [pltpu.VMEM(wide, kind)] * 2
        + [pltpu.VMEM(square, kind)] * 2,
        in_specs=[VMEM, VMEM] + [FAR] * 4,
        out_specs=[VMEM] * 7,
        scratch_shapes=[
            pltpu.VMEM(temporal_qkv.shape, kind),
            pltpu.VMEM(spatial_qkv.shape, kind),
            pltpu.VMEM(square, kind),
            pltpu.VMEM((groups, frames, SUB, channels), jnp.float32),
            pltpu.SemaphoreType.DMA((4,)),
        ],
        cost_estimate=pl.CostEstimate(
            flops=2 * count * channels * 3 * channels, bytes_accessed=4 << 20, transcendentals=0
        ),
        compiler_params=pltpu.CompilerParams(vmem_limit_bytes=LIMIT),
        name="local",
    )(
        latents,
        gain.reshape(1, channels),
        *(far(w) for w in (temporal_qkv, temporal_out, spatial_qkv, spatial_out)),
    )


def remote_pairs(dense, gain, tw_ref, normed_ref, pixels):
    channels = gain.shape[1]
    groups, slots = normed_ref.shape[:2]
    for j, frame in enumerate(dense):
        normed = layer_norm(unpack(frame, pixels, channels).astype(jnp.float32), gain)
        for g in range(groups):
            normed_ref[g, j] = normed[g * SUB : (g + 1) * SUB]
    for j in range(len(dense), slots):
        for g in range(groups):
            normed_ref[g, j] = jnp.zeros((SUB, channels), jnp.float32)
    whole = channels // LANES * LANES
    rows = normed_ref[...].reshape(groups * slots * SUB, channels).astype(jnp.bfloat16)
    return jnp.dot(rows, tw_ref[:, whole:], preferred_element_type=jnp.float32).astype(jnp.bfloat16)


def early_kernel(gain_ref, tw_ref, *rest):
    *refs, kv_ref, normed_ref = rest
    dense = [ref[i] for ref in refs for i in range(min(HALO, ref.shape[0]))]
    pixels = normed_ref.shape[0] * SUB
    kv_ref[...] = remote_pairs(dense, gain_ref[...], tw_ref, normed_ref, pixels)


def early(gain, weights, frames, pixels, slots):
    channels = weights.shape[0]
    groups = pixels // SUB
    kind = weights.dtype
    return pl.pallas_call(
        early_kernel,
        out_shape=pltpu.VMEM((pixels * slots, weights.shape[1] - channels // LANES * LANES), kind),
        in_specs=[VMEM] + [VMEM] * (1 + len(frames)),
        out_specs=VMEM,
        scratch_shapes=[pltpu.VMEM((groups, slots, SUB, channels), jnp.float32)],
        cost_estimate=pl.CostEstimate(
            flops=2 * pixels * slots * channels * 2 * channels, bytes_accessed=2 << 20, transcendentals=0
        ),
        compiler_params=pltpu.CompilerParams(vmem_limit_bytes=LIMIT),
        name="early",
    )(gain.reshape(1, channels), weights, *frames)


def temporal_kernel(
    clips, ahead, early_held, late_held, pix_count, cross,
    q_ref, own_ref, xg_ref, kv_ref, gain_ref, tw_ref, to_ref, *rest,
):
    halves = pix_count // 2
    scratch = 4 if cross else 2
    before_refs, rest = rest[:ahead], rest[ahead:]
    last_refs, sends, rest = (
        rest[: len(rest) - halves - scratch],
        rest[len(rest) - halves - scratch : len(rest) - scratch],
        rest[len(rest) - scratch :],
    )
    groups, frames, _, channels = xg_ref.shape
    pixels = groups * SUB
    _, _, first_there, second_there = neighbours(clips)
    if cross:
        late_ref, normed_ref, att_ref, rows_ref = rest
        dense = [ref[i] for ref in last_refs for i in range(HALO if ref.shape[0] == HALO + 1 else 0, ref.shape[0])]
        late_ref[...] = remote_pairs(dense, gain_ref[...], tw_ref, normed_ref, pixels)
    else:
        (late_ref,) = last_refs
        att_ref, rows_ref = rest
    place = lax.axis_index("pix")
    upper = place // halves
    half = 1 - upper if cross else upper
    whole = channels // LANES * LANES

    part = frames // 2
    mine, own = part * SUB, frames * SUB
    soon, more = kv_ref.shape[0] // groups, late_ref.shape[0] // groups
    sooner = sum(ref.shape[0] for ref in before_refs) // groups
    shape = (mine, own + sooner + soon + more)
    row = lax.broadcasted_iota(jnp.int32, shape, 0)
    column = lax.broadcasted_iota(jnp.int32, shape, 1)
    usable = lax.rem(row, SUB) == lax.rem(column, SUB)
    slot = (column - sooner) // SUB - frames
    usable &= (slot < 0) | (slot >= HALO) | first_there
    usable &= (slot < early_held) | (slot >= soon // SUB)
    usable &= (slot < soon // SUB) | (slot >= soon // SUB + HALO) | second_there
    usable &= slot < soon // SUB + late_held
    bias = jnp.where(usable, 0.0, NEG).astype(jnp.float32)

    blocks = [(g, tile) for g in range(groups) for tile in plan(channels)]

    def pairs_of(g, column):
        span = slice(column - whole, column - whole + LANES)
        return jnp.concatenate(
            [
                own_ref[g * own : (g + 1) * own, span],
                *(ref[g * sooner : (g + 1) * sooner, span] for ref in before_refs),
                kv_ref[g * soon : (g + 1) * soon, span],
                late_ref[g * more : (g + 1) * more, span],
            ],
            axis=0,
        )

    def score(i):
        g, tile = blocks[i]
        queries = q_ref[g, half, tile.head * mine : (tile.head + tile.held) * mine, :]
        scores = lax.dot_general(
            queries, pairs_of(g, tile.key), NT, preferred_element_type=jnp.float32
        )
        return scores + jnp.concatenate([bias] * tile.held, axis=0)

    def mix(i, weights, norm):
        g, tile = blocks[i]
        mixed = jnp.dot(weights, pairs_of(g, tile.value), preferred_element_type=jnp.float32) * norm
        att_ref[g * mine : (g + 1) * mine, tile.start : tile.start + tile.width] = unstack_heads(
            mixed, tile.held
        )[:, : tile.width].astype(jnp.bfloat16)

    pipelined(len(blocks), score, mix, LEAD)
    update = jnp.dot(att_ref[...], to_ref[...], preferred_element_type=jnp.float32)
    for g in range(groups):
        for f in range(part):
            at = (g * part + f) * SUB
            rows_ref[f, g * SUB : (g + 1) * SUB] = xg_ref[g, half * part + f] + update[at : at + SUB]
    per_device = sends[0].shape[0]
    for k, ref in enumerate(sends):
        target = jnp.bitwise_xor(lax.rem(place, halves), k)
        for i in range(per_device):
            ref[i] = pack(rows_ref[target * per_device + i].astype(jnp.bfloat16))


def temporal(
    parts, pairs, gain, weights, out_matrix, before, last, clips, early_held, late_held, pix_count, cross
):
    q, own, xg = parts
    groups, frames, _, channels = xg.shape
    pixels = groups * SUB
    count = frames * pixels
    kind = q.dtype
    dense = (pixels * channels // LANES, LANES)
    out_shape = [pltpu.VMEM((frames // pix_count,) + dense, kind)] * (pix_count // 2)
    scratch = [
        pltpu.VMEM((count // 2, channels), kind),
        pltpu.VMEM((frames // 2, pixels, channels), jnp.float32),
    ]
    if cross:
        slots = up(late_held, 2)
        out_shape = out_shape + [pltpu.VMEM((pixels * slots, pairs.shape[1]), kind)]
        scratch = [pltpu.VMEM((groups, slots, SUB, channels), jnp.float32)] + scratch
    return pl.pallas_call(
        functools.partial(temporal_kernel, clips, len(before), early_held, late_held, pix_count, cross),
        out_shape=out_shape,
        in_specs=[VMEM] * 4 + [VMEM] + [VMEM] * (2 + len(before) + len(last)),
        out_specs=[VMEM] * len(out_shape),
        scratch_shapes=scratch,
        cost_estimate=pl.CostEstimate(
            flops=2 * count * channels * 2 * channels, bytes_accessed=4 << 20, transcendentals=0
        ),
        compiler_params=pltpu.CompilerParams(vmem_limit_bytes=LIMIT),
        name="cross" if cross else "near",
    )(q, own, xg, pairs, gain.reshape(1, channels), weights, out_matrix, *before, *last)


def gather_rows(chunks, rows_ref, channels):
    halves = len(chunks)
    per_device, half_pixels = rows_ref.shape[:2]
    each = half_pixels // halves
    place = lax.rem(lax.axis_index("pix"), halves)
    for k, ref in enumerate(chunks):
        at = pl.multiple_of(jnp.bitwise_xor(place, k) * each, each)
        for i in range(per_device):
            rows_ref[i, pl.ds(at, each), :] = unpack(ref[i], each, channels).astype(jnp.float32)
    return rows_ref[...].reshape(per_device * half_pixels, channels)


def project_half(rows, gain, sw_ref):
    normed = layer_norm(rows, gain).astype(jnp.bfloat16)
    return jnp.dot(normed, sw_ref[...], preferred_element_type=jnp.float32).astype(jnp.bfloat16)


def ready_kernel(halves, gain_ref, sw_ref, *rest):
    chunks, (packed_ref, flipped_ref, rows_ref) = rest[:halves], rest[halves:]
    channels = sw_ref.shape[0]
    rows = gather_rows(chunks, rows_ref, channels)
    packed_ref[...] = project_half(rows, gain_ref[...], sw_ref)
    for i in range(rows_ref.shape[0]):
        flipped_ref[i] = rows_ref[i].T


def ready(gain, weights, chunks, pixels):
    halves = len(chunks)
    per_device = chunks[0].shape[0]
    channels = weights.shape[0]
    kind = chunks[0].dtype
    half = pixels // 2
    return pl.pallas_call(
        functools.partial(ready_kernel, halves),
        out_shape=[
            pltpu.VMEM((per_device * half, weights.shape[1]), kind),
            pltpu.VMEM((per_device, channels, half), jnp.float32),
        ],
        in_specs=[VMEM] + [VMEM] * (1 + halves),
        out_specs=[VMEM] * 2,
        scratch_shapes=[pltpu.VMEM((per_device, half, channels), jnp.float32)],
        cost_estimate=pl.CostEstimate(
            flops=2 * per_device * half * channels * 3 * channels,
            bytes_accessed=2 << 20,
            transcendentals=0,
        ),
        compiler_params=pltpu.CompilerParams(vmem_limit_bytes=LIMIT),
        name="ready",
    )(gain.reshape(1, channels), weights, *chunks)


def spatial_kernel(halves, gain_ref, sw_ref, so_ref, packed_ref, flipped_ref, *rest):
    chunks, (out_ref, rows_ref, att_ref) = rest[:halves], rest[halves:]
    per_device, channels, pixels = out_ref.shape
    half = pixels // 2
    rows = gather_rows(chunks, rows_ref, channels)
    late = project_half(rows, gain_ref[...], sw_ref)
    blocks = [
        (i, tile, sides)
        for i in range(per_device)
        for tile in plan(channels)
        for sides in SIDES
    ]

    def part_of(frame, column, sides):
        return jnp.concatenate(
            [
                (late if side else packed_ref)[
                    frame * half : (frame + 1) * half, column : column + LANES
                ]
                for side in sides
            ],
            axis=0,
        )

    def score(i):
        frame, tile, sides = blocks[i]
        return lax.dot_general(
            stack_heads(part_of(frame, tile.query, sides), tile.held),
            part_of(frame, tile.key, (0, 1)),
            NT,
            preferred_element_type=jnp.float32,
        )

    def mix(i, weights, norm):
        frame, tile, sides = blocks[i]
        values = part_of(frame, tile.value, (0, 1))
        mixed = jnp.dot(weights, values, preferred_element_type=jnp.float32) * norm
        first = sides[0] * half
        att_ref[frame, first : first + len(sides) * half, tile.start : tile.start + tile.width] = (
            unstack_heads(mixed, tile.held)[:, : tile.width].astype(jnp.bfloat16)
        )

    pipelined(len(blocks), score, mix, SPATIAL_LEAD)
    upper = lax.axis_index("pix") // halves
    for i in range(per_device):
        update = lax.dot_general(so_ref[...], att_ref[i], NT, preferred_element_type=jnp.float32)
        here = pl.multiple_of(upper * half, half)
        there = pl.multiple_of((1 - upper) * half, half)
        out_ref[i, :, pl.ds(here, half)] = (flipped_ref[i] + update[:, :half]).astype(jnp.bfloat16)
        out_ref[i, :, pl.ds(there, half)] = (rows_ref[i].T + update[:, half:]).astype(jnp.bfloat16)


def spatial(gain, weights, out_matrix, packed, flipped, chunks, pixels):
    halves = len(chunks)
    per_device = chunks[0].shape[0]
    channels = out_matrix.shape[0]
    kind = chunks[0].dtype
    return pl.pallas_call(
        functools.partial(spatial_kernel, halves),
        out_shape=jax.ShapeDtypeStruct((per_device, channels, pixels), kind),
        in_specs=[VMEM] + [VMEM] * (4 + halves),
        out_specs=pl.BlockSpec(),
        scratch_shapes=[
            pltpu.VMEM((per_device, pixels // 2, channels), jnp.float32),
            pltpu.VMEM((per_device, pixels, channels), kind),
        ],
        cost_estimate=pl.CostEstimate(
            flops=2 * per_device * pixels * channels * (4 * channels + 2 * pixels),
            bytes_accessed=4 << 20,
            transcendentals=0,
        ),
        compiler_params=pltpu.CompilerParams(vmem_limit_bytes=LIMIT),
        name="spatial",
    )(gain.reshape(1, channels), weights, out_matrix, packed, flipped, *chunks)


def both_ways(pairs, count):
    target = [device ^ 1 for device in range(count)]
    for a, b in pairs:
        target[a], target[b] = b, a
    return list(enumerate(target))


def border_pairs(clips, pix_count, turn):
    pairs = [
        (a * pix_count + place, (a + 1) * pix_count + place)
        for a in range(turn, clips - 1, 2)
        for place in range(pix_count)
    ]
    return both_ways(pairs, clips * pix_count)


def body(
    latents,
    sampled,
    temporal_gain,
    temporal_qkv,
    temporal_out,
    spatial_gain,
    spatial_qkv,
    spatial_out,
):
    clips, pix_count = lax.axis_size("clip"), lax.axis_size("pix")
    pixels = latents.shape[1] * pix_count
    gathered = clips > DIRECT_CLIPS or clips & (clips - 1) != 0
    x = pltpu.with_memory_space_constraint(latents, pltpu.VMEM)
    p = pick_frame(latents, sampled)
    a, b = prep(x, p, clips, not gathered)
    if gathered:
        soon, last = [], [lax.all_gather(p, "clip", axis=0, tiled=True)]
    else:
        soon, last = [], [p]
        for step in range(2, clips):
            pick = lax.ppermute(p, "clip", [(i, i ^ step) for i in range(clips)])
            (soon if step == 2 else last).append(pick)
    a = lax.ppermute(a, ("clip", "pix"), border_pairs(clips, pix_count, 0))
    b = lax.ppermute(b, ("clip", "pix"), border_pairs(clips, pix_count, 1))
    q, own, xg, tw, sw, to, so = local(
        x, temporal_gain, temporal_qkv, temporal_out, spatial_qkv, spatial_out
    )
    each, before = latents.shape[1], []
    if not gathered:
        before = [early(temporal_gain, tw, soon + last[:1], each, up(len(soon) + 1, 2))]
        last = last[1:] + [a]
    last = [b] + last
    late_held = sum(1 if part is a else part.shape[0] for part in last)
    pairs = early(temporal_gain, tw, [a], each, up(HALO, 2))
    rest = ((q, own, xg), pairs, temporal_gain, tw, to, before)
    held = (clips, HALO, late_held, pix_count)
    halves = pix_count // 2
    *sends, late = temporal(*rest, last, *held, True)

    def swap(chunk, step):
        return lax.ppermute(chunk, "pix", [(i, i ^ step) for i in range(pix_count)])

    crossed = [swap(sends[k], halves + k) for k in range(halves)]
    kept = temporal(*rest, [late], *held, False)
    here = [kept[0]] + [swap(kept[k], k) for k in range(1, halves)]
    packed, flipped = ready(spatial_gain, sw, here, pixels)
    return spatial(spatial_gain, sw, so, packed, flipped, crossed, pixels).transpose(0, 2, 1)


def solution(mesh):
    placed = (P(("group", "clip"), "pix", None), P(("group", "clip")), P(), P(), P(), P(), P(), P())
    return jax.shard_map(
        body,
        mesh=mesh,
        in_specs=placed,
        out_specs=P(("group", "clip", "pix"), None, None),
        check_vma=False,
    )
```
